256 devices in a mesh: lon: 8 (over y, x_lo), lat: 16 (over z, x_hi), rep: 2 (over core).
Axes of the slice: x: 4 (x_hi: 2, x_lo: 2; x = x_hi * 2 + x_lo), y: 4, z: 8, core: 2. Of those that a mesh axis runs over, the one named last changes fastest.
Arguments:
- forcing: float32 [8, 4, 2, 512, 2048], P('rep', None, None, 'lat', 'lon'), may hold values from -6 to 6
- diffusivity: float32 [512, 2048], P('lat', 'lon'), may hold values from 0.1 to 0.22
- ocean: int32 [512, 2048], P('lat', 'lon'), may hold values 0 or 1
- phase: float32 [4], replicated, may hold values from 0.1 to 0.4
- site_cell: int32 [16, 8, 2048], P('lat', 'lon'), may hold values from 0 to 8191
- site_count: int32 [16, 8], P('lat', 'lon'), may hold values from 1 to 2048, 10240 in all within a row
- site_weight: float32 [16, 8, 2048], P('lat', 'lon'), may hold values from 0.5 to 5
Outputs:
- representer: float32 [8, 4, 2, 512, 2048], P('rep', None, None, 'lat', 'lon')
- gram: float32 [8, 8], P('rep')
The draws below stay inside these ranges and needn't reach their ends.
Inputs may be any that keep to these rules, and one draw needn't show every extreme that they name: `site_count`: live slots are the first ones of a block; in each latitude row of blocks one block has all 2048 slots live.
All inputs are finite; a program needn't handle non-finite values. No bound on the sum of `ocean` on one device may be relied on, other than what follows from the above.
Results may differ from the reference program's by a relative error of at most 0.00007.
Values sent between devices are 32-bit elements; how exact they have to be, the bound alone decides.
A program may use at most 64 MiB of HBM per device.

```python
import math
import jax
import jax.numpy as jnp
import numpy as np
from jax import lax

CONST = 4
SWEEPS = 4
CLAT = 32
CLON = 256
SITE_DEV = 2048
NLAT = 512
NLON = 2048
REPS = 8
N_LON = 8
N_LAT = 16


def touch_ends(entries, stream_key, least, largest):
    index_at = [jax.random.randint(jax.random.fold_in(stream_key, axis), (), 0, length) for axis, length in enumerate(entries.shape)]
    longest = entries.shape.index(max(entries.shape))
    neighbour = index_at[:longest] + [(index_at[longest] + 1) % entries.shape[longest]] + index_at[longest + 1:]
    return entries.at[tuple(index_at)].set(least).at[tuple(neighbour)].set(largest)


def shard_levels(stream_key, extent, cuts, least, largest):
    loudness, own = 1.0, jax.random.fold_in(stream_key, 6)
    for dim, blocks in cuts:
        steps = jnp.exp(jax.random.uniform(jax.random.fold_in(own, dim), (blocks,), jnp.float32, least / len(cuts), largest / len(cuts)))
        loudness = loudness * jnp.repeat(steps, extent[dim] // blocks).reshape([-1 if axis == dim else 1 for axis in range(len(extent))])
    return loudness


def length_profile(number_of, total, reach, lean):
    weights = [(1 << 20) // math.isqrt(grade ** lean) + 1 for grade in range(2, number_of + 1)]
    spare, counts = total - reach - (number_of - 1), [1] * (number_of - 1)
    while spare > 0:
        free = [i for i in range(number_of - 1) if counts[i] < reach]
        pool, budget = sum([weights[i] for i in free]), spare
        for i in free:
            addition = min(reach - counts[i], max(1, budget * weights[i] // pool), spare)
            counts[i] = counts[i] + addition
            spare = spare - addition
    return np.array([reach] + counts)


def ragged_sizes(rng, amount, total, bound, slope):
    if amount == 2:
        one = jax.random.randint(rng, (), max(1, total - bound), min(bound, total - 1) + 1)
        return jnp.stack([one, total - one])
    lengths = jnp.asarray(length_profile(amount, total, bound, slope), jnp.int32)
    twos = (amount - 1) // 2
    source_of, taker = lengths[1:1 + 2 * twos:2], lengths[2:2 + 2 * twos:2]
    room = jnp.minimum(source_of - 1, bound - taker)
    moved = jax.random.randint(jax.random.fold_in(rng, 1), (twos,), 0, 1 << 20) % (room + 1)
    lengths = lengths.at[1:1 + 2 * twos:2].set(source_of - moved).at[2:2 + 2 * twos:2].set(taker + moved)
    return lengths[jax.random.permutation(jax.random.fold_in(rng, 2), amount)]


def bell_draw(key, dims, deviation, reach, pieces=(), kind=jnp.bfloat16):
    entries = jax.random.normal(key, dims, jnp.float32) * deviation
    if len(pieces) > 0:
        entries = shard_levels(key, dims, pieces, -0.22, 0.18) * entries
    return jnp.clip(entries, min=-reach, max=reach).astype(kind)


def setup_inputs(seed: int = 0) -> dict:
    arg_keys = jax.random.split(jax.random.key(seed), 8)
    return {
        "forcing": bell_draw(arg_keys[0], (REPS, CONST, 2, NLAT, NLON), 1.0, 6.0, ((0, 2), (3, 16), (4, 8)), jnp.float32),
        "diffusivity": jnp.clip(jnp.exp(math.log(0.22) - 0.78845734 * jax.random.uniform(arg_keys[1], (NLAT, NLON), jnp.float32) ** shard_levels(arg_keys[1], (NLAT, NLON), ((0, 16), (1, 8)), -0.2, 0.2)), 0.1, 0.22),
        "ocean": touch_ends((jax.random.randint(arg_keys[2], (NLAT, NLON), 0, 8) < 7).astype(jnp.int32), jax.random.fold_in(arg_keys[2], 1), 0, 1),
        "phase": jnp.clip(jax.random.uniform(arg_keys[3], (CONST,), jnp.float32, 0.1, 0.4), 0.1, 0.4),
        "site_cell": touch_ends(jax.random.randint(arg_keys[4], (N_LAT, N_LON, SITE_DEV), 0, CLAT * CLON), jax.random.fold_in(arg_keys[4], 1), 0, (CLAT * CLON) - 1).astype(jnp.int32),
        "site_count": jax.vmap(lambda own: ragged_sizes(own, N_LON, N_LON * SITE_DEV * 5 // 8, SITE_DEV, 2))(jax.random.split(arg_keys[5], N_LAT)).reshape((N_LAT, N_LON)).astype(jnp.int32),
        "site_weight": jnp.clip(jnp.exp(math.log(5.0) - 2.3025851 * jax.random.uniform(arg_keys[6], (N_LAT, N_LON, SITE_DEV), jnp.float32) ** shard_levels(arg_keys[6], (N_LAT, N_LON, SITE_DEV), ((0, 16), (1, 8)), -0.2, 0.2)), 0.5, 5.0),
    }


DAMPING = 0.9


def laplace(values):
    widths = [(0, 0)] * (values.ndim - 2) + [(1, 1), (0, 0)]
    padded = jnp.pad(values, widths)
    north = padded[..., 2:, :]
    south = padded[..., :-2, :]
    east = jnp.roll(values, -1, axis=-1)
    west = jnp.roll(values, 1, axis=-1)
    return north + south + east + west - 4.0 * values


def rotate(field, cosine, sinus):
    real_part = field[:, 0]
    imag_part = field[:, 1]
    new_real = cosine * real_part - sinus * imag_part
    new_imag = sinus * real_part + cosine * imag_part
    return jnp.stack([new_real, new_imag], axis=1)


def reference(forcing, diffusivity, ocean, phase, site_cell, site_count, site_weight):
    wet = ocean.astype(jnp.float32)
    cosine = jnp.cos(phase)[:, None, None]
    sinus = jnp.sin(phase)[:, None, None]

    def sweep_all(field):
        for step in range(SWEEPS):
            field = wet * (DAMPING * rotate(field, cosine, -sinus) + laplace(diffusivity * field))
        for step in range(SWEEPS):
            field = wet * (DAMPING * rotate(field, cosine, sinus) + diffusivity * laplace(field))
        return field

    representer = lax.map(sweep_all, forcing)
    block_lat = jnp.arange(N_LAT, dtype=jnp.int32)[:, None, None]
    block_lon = jnp.arange(N_LON, dtype=jnp.int32)[None, :, None]
    cell_lat = block_lat * CLAT + site_cell // CLON
    cell_lon = block_lon * CLON + site_cell % CLON
    global_cell = (cell_lat * NLON + cell_lon).reshape(-1)
    slots = jnp.arange(SITE_DEV, dtype=jnp.int32)[None, None, :]
    live = (slots < site_count[:, :, None]).astype(jnp.float32)
    weight = (site_weight * live).reshape(-1)
    flat = representer.reshape(REPS, CONST * 2, NLAT * NLON)
    samples = jnp.take(flat, global_cell, axis=2)
    weighted = (samples * weight[None, None, :]).reshape(REPS, -1)
    plain = samples.reshape(REPS, -1)
    gram = jnp.dot(weighted, plain.T, precision=lax.Precision.HIGHEST, preferred_element_type=jnp.float32)
    gram = gram / float(N_LAT * N_LON * SITE_DEV)
    return representer, gram
```

```python
import functools

import jax
import jax.numpy as jnp
import numpy as np
from jax import lax
from jax.experimental import pallas as pl
from jax.experimental.pallas import tpu as pltpu
from jax.sharding import PartitionSpec as P

CONST = 4
SWEEPS = 4
DAMPING = 0.9
MESH = pl.DeviceIdType.MESH

DEPTH = 2 * SWEEPS
GROUPS = 2
LANES = 128
OWN_PAIRS = ((0, 0), (1, 1), (0, 1))
CROSS_PAIRS = ((0, 0), (0, 1), (1, 0), (1, 1))


def entry_lanes(rep, row, col):
    a, ra = divmod(row, 2)
    group, local = divmod(col, 4)
    b, rb = divmod(local, 2)
    if group == rep:
        if a > b:
            a, ra, b, rb = b, rb, a, ra
        at = OWN_PAIRS.index((a, b)) * 2 + (ra != rb)
        return [32 * rep + 16 * rb + at]
    first = 6 + CROSS_PAIRS.index((a, b)) * 2 + (ra != rb)
    second = 6 + CROSS_PAIRS.index((b, a)) * 2 + (ra != rb)
    return [32 * rep + 16 * rb + first, 32 * group + 16 * ra + second]


def entry_masks(scale):
    masks = np.zeros((2, 8, 8, LANES), np.float32)
    for rep in range(2):
        for row in range(4):
            for col in range(8):
                for lane in entry_lanes(rep, row, col):
                    masks[rep, col, row, lane] = 1.0 / scale
    return masks


def kernel(
    n_lon,
    n_lat,
    planes_hbm,
    flat_hbm,
    diff_hbm,
    ocean_hbm,
    cell_hbm,
    weight_hbm,
    masks_hbm,
    phase,
    count,
    rep_out,
    gram_out,
    raw,
    out_buf,
    field,
    halo_n,
    halo_s,
    pack,
    east,
    west,
    coef,
    ocean,
    coef_main,
    coef_east,
    coef_west,
    diff_b,
    wet_b,
    trig,
    cell,
    weight,
    masks,
    grid_w,
    partner,
    acc,
    stage1,
    stage2,
    local_sem,
    out_sem,
    lat_send,
    lat_recv,
    lon_send,
    lon_recv,
    corner_send,
    corner_recv,
    coef_send,
    coef_recv,
    part_send,
    part_recv,
    sum1_send,
    sum1_recv,
    sum2_send,
    sum2_recv,
):
    rows, cols = diff_hbm.shape
    i_lon, i_lat, i_rep = lax.axis_index("lon"), lax.axis_index("lat"), lax.axis_index("rep")

    def at(d_lon, d_lat):
        return (
            lax.rem(i_lon + n_lon + d_lon, n_lon),
            lax.rem(i_lat + n_lat + d_lat, n_lat),
            i_rep,
        )

    other = (i_lon, i_lat, 1 - i_rep)
    size1, size2 = n_lat, 2 * n_lon
    i_z, i_half = i_lat // 2, lax.rem(i_lat, 2)
    me1 = i_z * 2 + i_rep
    me2 = i_half * n_lon + i_lon

    def peer1(index):
        return (i_lon, (index // 2) * 2 + i_half, lax.rem(index, 2))

    def peer2(index):
        return (lax.rem(index, n_lon), i_z * 2 + index // n_lon, i_rep)

    neighbours = [(a, b) for a in (-1, 0, 1) for b in (-1, 0, 1) if (a, b) != (0, 0)]

    loads = [
        pltpu.make_async_copy(diff_hbm, coef.at[0], local_sem.at[0]),
        pltpu.make_async_copy(ocean_hbm, ocean, local_sem.at[1]),
        pltpu.make_async_copy(cell_hbm, cell, local_sem.at[2]),
        pltpu.make_async_copy(weight_hbm, weight, local_sem.at[3]),
        pltpu.make_async_copy(masks_hbm, masks, local_sem.at[4]),
    ]
    loads += [
        pltpu.make_async_copy(
            flat_hbm.at[:, pl.ds(t * LANES, LANES)], raw.at[t], local_sem.at[5 + t]
        )
        for t in range(cols // LANES)
    ]
    for load in loads[5:] + loads[:5]:
        load.start()

    barrier = pltpu.get_barrier_semaphore()
    for a, b in neighbours:
        pl.semaphore_signal(barrier, inc=1, device_id=at(a, b), device_id_type=MESH)
    for k in range(1, size1):
        pl.semaphore_signal(
            barrier, inc=1, device_id=peer1(lax.rem(me1 + k, size1)), device_id_type=MESH
        )
    for k in range(1, size2):
        pl.semaphore_signal(
            barrier, inc=1, device_id=peer2(lax.rem(me2 + k, size2)), device_id_type=MESH
        )

    lane = lax.broadcasted_iota(jnp.int32, (8, LANES), 1)
    sub = lax.broadcasted_iota(jnp.int32, (8, LANES), 0)
    angle = jnp.zeros((8, LANES), jnp.float32)
    for c in range(CONST):
        angle = jnp.where(lax.rem(sub, CONST) == c, phase[c], angle)
    trig[0] = DAMPING * jnp.cos(angle)
    trig[1] = DAMPING * jnp.sin(angle)

    loads[0].wait()
    loads[1].wait()
    coef[1] = ocean[...].astype(jnp.float32)
    for load in loads[5:]:
        load.wait()

    def raw_row(ref, rh, p, row, tile):
        start = (16 * rh + p) * rows + row
        return ref[tile, pl.ds(start, 8, stride=2 * rows), :]

    slot = lane // DEPTH
    last = cols // LANES - 1

    def pack_half(index, carry):
        rh, rb = index // 2, lax.rem(index, 2)
        for p in range(2):
            to_west = jnp.zeros((8, LANES), jnp.float32)
            to_east = jnp.zeros((8, LANES), jnp.float32)
            for k in range(16):
                left = raw_row(raw, rh, p, rb * 16 + k, 0)
                right = raw_row(raw, rh, p, rb * 16 + k, last)
                if k:
                    left = pltpu.roll(left, DEPTH * k, 1)
                if k < 15:
                    right = pltpu.roll(right, DEPTH * (k + 1), 1)
                to_west = jnp.where(slot == k, left, to_west)
                to_east = jnp.where(slot == k, right, to_east)
            pack[0, rb, rh, p] = to_west
            pack[1, rb, rh, p] = to_east
        return carry

    lax.fori_loop(0, 4, pack_half, 0)

    pl.semaphore_wait(barrier, len(neighbours) + size1 - 1 + size2 - 1)

    def send(src, dst, sends, recvs, index, device):
        copy = pltpu.make_async_remote_copy(
            src, dst, sends.at[index], recvs.at[index], device_id=device, device_id_type=MESH
        )
        copy.start()
        return copy

    top, low = pl.ds(0, DEPTH), pl.ds(rows - DEPTH, DEPTH)
    body, head, tail = pl.ds(DEPTH, rows), pl.ds(0, DEPTH), pl.ds(rows + DEPTH, DEPTH)
    left_tile, right_tile = pl.ds(0, LANES), pl.ds(cols - LANES, LANES)
    lon_copies = [
        send(pack.at[0], east.at[pl.ds(1, 2)], lon_send, lon_recv, 0, at(-1, 0)),
        send(pack.at[1], west.at[pl.ds(1, 2)], lon_send, lon_recv, 1, at(1, 0)),
    ]
    coef_lon = [
        send(coef.at[:, :, left_tile], coef_east.at[:, body], coef_send, coef_recv, 0, at(-1, 0)),
        send(coef.at[:, :, right_tile], coef_west.at[:, body], coef_send, coef_recv, 1, at(1, 0)),
    ]
    lat_copies = []
    for rh in range(GROUPS):
        pair = []
        for side, (src, dst, hop) in enumerate(((low, halo_n, 1), (top, halo_s, -1))):
            for t in range(cols // LANES):
                pair.append(
                    send(
                        planes_hbm.at[pl.ds(16 * rh, 16), src, pl.ds(t * LANES, LANES)],
                        dst.at[rh, t].reshape(16, DEPTH, LANES),
                        lat_send,
                        lat_recv,
                        4 * rh + 2 * side + t,
                        at(0, hop),
                    )
                )
        lat_copies.append(pair)
    coef_rest = [
        send(coef.at[:, low], coef_main.at[:, head], coef_send, coef_recv, 2, at(0, 1)),
        send(coef.at[:, top], coef_main.at[:, tail], coef_send, coef_recv, 3, at(0, -1)),
        send(
            coef.at[:, low, left_tile], coef_east.at[:, head], coef_send, coef_recv, 4, at(-1, 1)
        ),
        send(
            coef.at[:, top, left_tile], coef_east.at[:, tail], coef_send, coef_recv, 5, at(-1, -1)
        ),
        send(
            coef.at[:, low, right_tile], coef_west.at[:, head], coef_send, coef_recv, 6, at(1, 1)
        ),
        send(
            coef.at[:, top, right_tile], coef_west.at[:, tail], coef_send, coef_recv, 7, at(1, -1)
        ),
    ]
    corner_copies = [
        send(pack.at[0, 1], east.at[0], corner_send, corner_recv, 0, at(-1, 1)),
        send(pack.at[0, 0], east.at[3], corner_send, corner_recv, 1, at(-1, -1)),
        send(pack.at[1, 1], west.at[0], corner_send, corner_recv, 2, at(1, 1)),
        send(pack.at[1, 0], west.at[3], corner_send, corner_recv, 3, at(1, -1)),
    ]

    loads[2].wait()
    loads[3].wait()
    live_slots = count[0, 0]
    row_id = lax.broadcasted_iota(jnp.int32, (rows, LANES), 0)
    col_id = lax.broadcasted_iota(jnp.int32, (cols, LANES), 0)
    lane_1 = lax.broadcasted_iota(jnp.int32, (1, LANES), 1)

    def add_sites(j, total):
        cells = cell[pl.ds(j, 1), :]
        value = jnp.where(j * LANES + lane_1 < live_slots, weight[pl.ds(j, 1), :], 0.0)
        one = value.astype(jnp.bfloat16)
        rest = value - one.astype(jnp.float32)
        two = rest.astype(jnp.bfloat16)
        three = rest - two.astype(jnp.float32)
        hit_row = jnp.broadcast_to(cells // cols, (rows, LANES)) == row_id
        hit_col = jnp.broadcast_to(lax.rem(cells, cols), (cols, LANES)) == col_id
        terms = [
            jnp.where(hit_row, jnp.broadcast_to(term.astype(jnp.float32), (rows, LANES)), 0.0)
            for term in (one, two, three)
        ]
        lhs = jnp.concatenate(terms, axis=0).astype(jnp.bfloat16)
        rhs = jnp.where(hit_col, 1.0, 0.0).astype(jnp.bfloat16)
        return total + lax.dot_general(
            lhs, rhs, (((1,), (1,)), ((), ())), preferred_element_type=jnp.float32
        )

    summed = lax.fori_loop(
        0, cell.shape[0], add_sites, jnp.zeros((3 * rows, cols), jnp.float32)
    )
    summed = summed[:rows] + summed[rows : 2 * rows] + summed[2 * rows :]
    for row in range(rows):
        grid_w[row] = jnp.broadcast_to(summed[row : row + 1], (8, cols))

    def spread(ext, valid):
        for j, dst in enumerate((diff_b, wet_b)):
            far = jnp.where(lane < DEPTH, coef_east[j, pl.ds(ext, 8)], coef_west[j, pl.ds(ext, 8)])
            far = jnp.where((lane < DEPTH) | (lane >= LANES - DEPTH), far, 0.0)
            tiles = [
                coef_main[j, pl.ds(ext, 8), t * LANES : (t + 1) * LANES]
                for t in range(cols // LANES)
            ] + [far]
            for t, tile in enumerate(tiles):
                if valid is not None:
                    tile = jnp.where(valid, tile, 0.0)
                for i in range(8):
                    dst[ext + i, :, t * LANES : (t + 1) * LANES] = jnp.broadcast_to(
                        tile[i : i + 1], (8, LANES)
                    )

    def far_tile(ext, rb, k, rh, p):
        right = east[rb, rh, p]
        left = west[rb, rh, p]
        if k:
            right = pltpu.roll(right, LANES - DEPTH * k, 1)
        if (LANES - DEPTH - DEPTH * k) % LANES:
            left = pltpu.roll(left, LANES - DEPTH - DEPTH * k, 1)
        field[0, rh, p, ext, :, cols : cols + LANES] = jnp.where(lane < LANES // 2, right, left)

    def unpack_body(index, carry):
        rh, rb = index // 2, lax.rem(index, 2)
        for p in range(2):
            for k in range(16):
                row = rb * 16 + k
                for t in range(cols // LANES):
                    field[0, rh, p, DEPTH + row, :, t * LANES : (t + 1) * LANES] = raw_row(
                        raw, rh, p, row, t
                    )
                far_tile(DEPTH + row, rb + 1, k, rh, p)
        return carry

    def unpack_edges(rh):
        for p in range(2):
            for i in range(DEPTH):
                for side, (halo, ext, rb, k) in enumerate(
                    ((halo_n, i, 0, 8 + i), (halo_s, rows + DEPTH + i, 3, i))
                ):
                    for t in range(cols // LANES):
                        at_lanes = slice(t * LANES, (t + 1) * LANES)
                        field[0, rh, p, ext, :, at_lanes] = halo[
                            rh, t, pl.ds(p * DEPTH + i, 8, stride=2 * DEPTH), :
                        ]
                    far_tile(ext, rb, k, rh, p)

    tiles = cols // LANES + 1

    def chunk(src, dst, rh, ext, transposed, final):
        cosine = trig[0]
        sinus = trig[1] if transposed else -trig[1]

        def tile_at(ref, index, t):
            return ref[index + (slice(None), slice(t * LANES, (t + 1) * LANES))]

        value = [
            [[tile_at(field, (src, rh, p, ext + i), t) for t in range(tiles)] for p in range(2)]
            for i in range(-1, 9)
        ]
        if transposed:
            coupling = [
                [tile_at(diff_b, (ext + i,), t) for t in range(tiles)] for i in range(-1, 9)
            ]
            spreads = [
                [[coupling[i][t] * value[i][p][t] for t in range(tiles)] for p in range(2)]
                for i in range(10)
            ]
        else:
            coupling = [None] + [
                [tile_at(diff_b, (ext + i,), t) for t in range(tiles)] for i in range(8)
            ]
            spreads = value
        for i in range(1, 9):
            around = []
            for p in range(2):
                here = spreads[i][p]
                to_right = [pltpu.roll(here[t], 1, 1) for t in range(tiles)]
                to_left = [pltpu.roll(here[t], LANES - 1, 1) for t in range(tiles)]
                total = []
                for t in range(tiles - 1 if final else tiles):
                    w = jnp.where(lane == 0, to_right[(t - 1) % tiles], to_right[t])
                    e = jnp.where(lane == LANES - 1, to_left[(t + 1) % tiles], to_left[t])
                    total.append((spreads[i - 1][p][t] + spreads[i + 1][p][t]) + (e + w))
                around.append(total)
            for t in range(tiles - 1 if final else tiles):
                wet = tile_at(wet_b, (ext + i - 1,), t)
                own = cosine - 4.0 * coupling[i][t]
                real, imag = value[i][0][t], value[i][1][t]
                sums = [around[p][t] for p in range(2)]
                if not transposed:
                    sums = [coupling[i][t] * v for v in sums]
                results = (
                    wet * ((own * real + sinus * imag) + sums[0]),
                    wet * ((own * imag - sinus * real) + sums[1]),
                )
                at_lanes = slice(t * LANES, (t + 1) * LANES)
                for p, result in enumerate(results):
                    field[dst, rh, p, ext + i - 1, :, at_lanes] = result
                    if final:
                        start = (16 * rh + p) * rows + (ext + i - 1 - DEPTH)
                        out_buf[t, pl.ds(start, 8, stride=2 * rows), :] = result

    def interior(step, transposed, final):
        chunks = (rows - 2 * step + 7) // 8

        def one(index, carry):
            rh, k = index // chunks, lax.rem(index, chunks)
            start = jnp.minimum(step + 8 * k, rows - 8 - step)
            chunk(lax.rem(step + 1, 2), lax.rem(step, 2), rh, DEPTH + start, transposed, final)
            return carry

        lax.fori_loop(0, GROUPS * chunks, one, 0)

    def edges(step, rh, transposed, final):
        src, dst = lax.rem(step + 1, 2), lax.rem(step, 2)
        chunk(src, dst, rh, step, transposed, final)
        chunk(src, dst, rh, rows + DEPTH - step, transposed, final)

    def loop(first, stop, body):
        def one(step, carry):
            body(step)
            return carry

        lax.fori_loop(first, stop, one, 0)

    coef_main[:, body] = coef[...]
    for copy in coef_lon:
        copy.wait_recv()
    for ext in range(DEPTH, DEPTH + rows, 8):
        spread(ext, None)
    for copy in lon_copies:
        copy.wait_recv()
    lax.fori_loop(0, 4, unpack_body, 0)
    loop(1, SWEEPS + 1, lambda step: interior(step, True, False))
    loop(SWEEPS + 1, DEPTH, lambda step: interior(step, False, False))
    interior(DEPTH, False, True)

    def share(rh, first, length, index):
        return send(
            field.at[0, rh, 1 - i_rep, pl.ds(DEPTH + first, length), :, pl.ds(0, cols)],
            partner.at[rh, pl.ds(first, length)],
            part_send,
            part_recv,
            index,
            other,
        )

    def put_rows(first, length, index):
        copies = []
        for t in range(cols // LANES):
            copy = pltpu.make_async_copy(
                out_buf.at[t].reshape(rep_out.shape[0], rows, LANES).at[:, pl.ds(first, length)],
                rep_out.at[:, pl.ds(first, length), pl.ds(t * LANES, LANES)],
                out_sem.at[index * (cols // LANES) + t],
            )
            copy.start()
            copies.append(copy)
        return copies

    stores = put_rows(DEPTH, rows - 2 * DEPTH, 0)
    parts = [share(rh, DEPTH, rows - 2 * DEPTH, rh) for rh in range(GROUPS)]
    acc[...] = jnp.zeros_like(acc)

    def own_rows(first, length):
        def one(row, totals):
            totals = list(totals)
            for p in range(2):
                for t in range(cols // LANES):
                    at_lanes = slice(t * LANES, (t + 1) * LANES)
                    values = [field[0, rh, p, DEPTH + row, :, at_lanes] for rh in range(GROUPS)]
                    scaled = [grid_w[row, :, at_lanes] * v for v in values]
                    turned = [pltpu.roll(v, 4, 0) for v in scaled]
                    for j, (a, b) in enumerate(OWN_PAIRS):
                        totals[2 * j] += scaled[a] * values[b]
                        totals[2 * j + 1] += turned[a] * values[b]
            return tuple(totals)

        totals = lax.fori_loop(first, first + length, one, tuple(acc[j] for j in range(6)))
        for j in range(6):
            acc[j] = totals[j]

    def cross_rows(first, length):
        def one(row, totals):
            totals = list(totals)
            for t in range(cols // LANES):
                at_lanes = slice(t * LANES, (t + 1) * LANES)
                scaled = [
                    grid_w[row, :, at_lanes] * field[0, rh, i_rep, DEPTH + row, :, at_lanes]
                    for rh in range(GROUPS)
                ]
                turned = [pltpu.roll(v, 4, 0) for v in scaled]
                values = [partner[rh, row, :, at_lanes] for rh in range(GROUPS)]
                for j, (a, b) in enumerate(CROSS_PAIRS):
                    totals[2 * j] += scaled[a] * values[b]
                    totals[2 * j + 1] += turned[a] * values[b]
            return tuple(totals)

        totals = lax.fori_loop(first, first + length, one, tuple(acc[6 + j] for j in range(8)))
        for j in range(8):
            acc[6 + j] = totals[j]

    own_rows(DEPTH, rows - 2 * DEPTH)
    for copy in parts:
        copy.wait_recv()
    cross_rows(DEPTH, rows - 2 * DEPTH)

    for copy in coef_rest:
        copy.wait_recv()
    spread(0, i_lat > 0)
    spread(rows + DEPTH, i_lat < n_lat - 1)
    for copy in corner_copies:
        copy.wait_recv()
    late = []
    for rh in range(GROUPS):
        for copy in lat_copies[rh]:
            copy.wait_recv()
        unpack_edges(rh)
        loop(1, SWEEPS + 1, lambda step: edges(step, rh, True, False))
        loop(SWEEPS + 1, DEPTH, lambda step: edges(step, rh, False, False))
        edges(DEPTH, rh, False, True)
        late.append(share(rh, 0, DEPTH, 2 + 2 * rh))
        late.append(share(rh, rows - DEPTH, DEPTH, 3 + 2 * rh))
    stores += put_rows(0, DEPTH, 1)
    stores += put_rows(rows - DEPTH, DEPTH, 2)
    own_rows(0, DEPTH)
    own_rows(rows - DEPTH, DEPTH)
    for copy in late:
        copy.wait_recv()
    cross_rows(0, DEPTH)
    cross_rows(rows - DEPTH, DEPTH)

    packed = jnp.zeros((8, LANES), jnp.float32)
    for j in range(14):
        packed = jnp.where(lane == j, jnp.sum(acc[j], axis=1, keepdims=True), packed)
    packed = packed + pltpu.roll(packed, 7, 0)
    packed = packed + pltpu.roll(packed, 6, 0)
    second = pltpu.roll(pltpu.roll(packed, 4, 0), 16, 1)
    packed = jnp.where(lane < 16, packed, second)
    packed = jnp.where(i_rep == 0, packed, pltpu.roll(packed, 32, 1))

    def sum_over(row, buffer, me, size, peer, sends, recvs):
        buffer[me] = row
        copies = []
        for k in range(1, size):
            target = lax.rem(me + k, size)
            copy = pltpu.make_async_remote_copy(
                buffer.at[me],
                buffer.at[me],
                sends.at[target],
                recvs.at[me],
                device_id=peer(target),
                device_id_type=MESH,
            )
            copy.start()
            copies.append(copy)
        for k in range(1, size):
            source = lax.rem(me + k, size)
            pltpu.make_async_remote_copy(
                buffer.at[source],
                buffer.at[source],
                sends.at[source],
                recvs.at[source],
                device_id=peer(source),
                device_id_type=MESH,
            ).wait_recv()
        total = buffer[0]
        for k in range(1, size):
            total = total + buffer[k]
        return total, copies

    row, sum1 = sum_over(packed[0:1], stage1, me1, size1, peer1, sum1_send, sum1_recv)
    row, sum2 = sum_over(row, stage2, me2, size2, peer2, sum2_send, sum2_recv)

    loads[4].wait()
    row = jnp.broadcast_to(row, (8, LANES))
    result = jnp.zeros((8, LANES), jnp.float32)
    for q in range(8):
        result = jnp.where(
            lane == q, jnp.sum(row * masks[i_rep, q], axis=1, keepdims=True), result
        )
    gram_out[...] = result[0:4, 0:8]

    for copy in lon_copies + coef_lon + coef_rest + corner_copies + parts + late + sum1 + sum2:
        copy.wait_send()
    for pair in lat_copies:
        for copy in pair:
            copy.wait_send()
    for copy in stores:
        copy.wait()


def local(n_lon, n_lat, forcing, diffusivity, ocean, phase, site_cell, site_count, site_weight):
    reps, const, parts, rows, cols = forcing.shape
    planes = reps * const * parts
    slots = site_cell.shape[2]
    masks = jnp.asarray(entry_masks(float(n_lon * n_lat * slots)))
    ext = rows + 2 * DEPTH
    wide = cols + LANES
    any_space = pl.BlockSpec(memory_space=pl.ANY)
    vmem = pl.BlockSpec(memory_space=pltpu.VMEM)
    smem = pl.BlockSpec(memory_space=pltpu.SMEM)
    f32 = jnp.float32
    dma = pltpu.SemaphoreType.DMA
    size1, size2 = n_lat, 2 * n_lon
    representer, gram = pl.pallas_call(
        functools.partial(kernel, n_lon, n_lat),
        out_shape=(
            jax.ShapeDtypeStruct((planes, rows, cols), f32),
            jax.ShapeDtypeStruct((reps, 2 * reps), f32),
        ),
        in_specs=[any_space] * 7 + [smem] * 2,
        out_specs=(any_space, vmem),
        scratch_shapes=[
            pltpu.VMEM((cols // LANES, planes * rows, LANES), f32),
            pltpu.VMEM((cols // LANES, planes * rows, LANES), f32),
            pltpu.VMEM((2, GROUPS, 2, ext, 8, wide), f32),
            pltpu.VMEM((GROUPS, cols // LANES, 16 * DEPTH, LANES), f32),
            pltpu.VMEM((GROUPS, cols // LANES, 16 * DEPTH, LANES), f32),
            pltpu.VMEM((2, 2, GROUPS, 2, 8, LANES), f32),
            pltpu.VMEM((4, GROUPS, 2, 8, LANES), f32),
            pltpu.VMEM((4, GROUPS, 2, 8, LANES), f32),
            pltpu.VMEM((2, rows, cols), f32),
            pltpu.VMEM((rows, cols), jnp.int32),
            pltpu.VMEM((2, ext, cols), f32),
            pltpu.VMEM((2, ext, LANES), f32),
            pltpu.VMEM((2, ext, LANES), f32),
            pltpu.VMEM((ext, 8, wide), f32),
            pltpu.VMEM((ext, 8, wide), f32),
            pltpu.VMEM((2, 8, LANES), f32),
            pltpu.VMEM((slots // LANES, LANES), jnp.int32),
            pltpu.VMEM((slots // LANES, LANES), f32),
            pltpu.VMEM(masks.shape, f32),
            pltpu.VMEM((rows, 8, cols), f32),
            pltpu.VMEM((GROUPS, rows, 8, cols), f32),
            pltpu.VMEM((14, 8, LANES), f32),
            pltpu.VMEM((size1, 1, LANES), f32),
            pltpu.VMEM((size2, 1, LANES), f32),
            dma((5 + cols // LANES,)),
            dma((3 * cols // LANES,)),
            dma((4 * cols // LANES,)),
            dma((4 * cols // LANES,)),
            dma((2,)),
            dma((2,)),
            dma((4,)),
            dma((4,)),
            dma((8,)),
            dma((8,)),
            dma((6,)),
            dma((6,)),
            dma((size1,)),
            dma((size1,)),
            dma((size2,)),
            dma((size2,)),
        ],
        compiler_params=pltpu.CompilerParams(
            collective_id=0, has_side_effects=True, vmem_limit_bytes=48 << 20
        ),
        name="representer_block",
    )(
        forcing.reshape(planes, rows, cols),
        forcing.reshape(planes * rows, cols),
        diffusivity,
        ocean,
        site_cell.reshape(slots // LANES, LANES),
        site_weight.reshape(slots // LANES, LANES),
        masks,
        phase,
        site_count,
    )
    return representer.reshape(forcing.shape), gram


def solution(mesh):
    return jax.shard_map(
        functools.partial(local, mesh.shape["lon"], mesh.shape["lat"]),
        mesh=mesh,
        in_specs=(
            P("rep", None, None, "lat", "lon"),
            P("lat", "lon"),
            P("lat", "lon"),
            P(),
            P("lat", "lon", None),
            P("lat", "lon"),
            P("lat", "lon", None),
        ),
        out_specs=(P("rep", None, None, "lat", "lon"), P("rep", None)),
        check_vma=False,
    )
```

```python
import functools

import jax
import jax.numpy as jnp
import numpy as np
from jax import lax
from jax.experimental import pallas as pl
from jax.experimental.pallas import tpu as pltpu
from jax.sharding import PartitionSpec as P

CONST = 4
SWEEPS = 4
DAMPING = 0.9
MESH = pl.DeviceIdType.MESH

DEPTH = 2 * SWEEPS
GROUPS = 2
LANES = 128
OWN_PAIRS = ((0, 0), (1, 1), (0, 1))
CROSS_PAIRS = ((0, 0), (0, 1), (1, 0), (1, 1))


def entry_lanes(rep, row, col):
    a, ra = divmod(row, 2)
    group, local = divmod(col, 4)
    b, rb = divmod(local, 2)
    if group == rep:
        if a > b:
            a, ra, b, rb = b, rb, a, ra
        at = OWN_PAIRS.index((a, b)) * 2 + (ra != rb)
        return [32 * rep + 16 * rb + at]
    first = 6 + CROSS_PAIRS.index((a, b)) * 2 + (ra != rb)
    second = 6 + CROSS_PAIRS.index((b, a)) * 2 + (ra != rb)
    return [32 * rep + 16 * rb + first, 32 * group + 16 * ra + second]


def entry_masks(scale):
    masks = np.zeros((2, 8, 8, LANES), np.float32)
    for rep in range(2):
        for row in range(4):
            for col in range(8):
                for lane in entry_lanes(rep, row, col):
                    masks[rep, col, row, lane] = 1.0 / scale
    return masks


def kernel(
    n_lon,
    n_lat,
    planes_hbm,
    diff_hbm,
    ocean_hbm,
    cell_hbm,
    weight_hbm,
    masks_hbm,
    phase_hbm,
    count_hbm,
    rep_out,
    gram_out,
    start,
    odd,
    even,
    strip_start,
    strip_odd,
    strip_even,
    pack,
    east,
    west,
    coef,
    ocean,
    coef_lat,
    factor,
    trig,
    cell,
    weight,
    masks,
    phase,
    count,
    grid_w,
    partner,
    acc,
    stage1,
    stage2,
    load_sem,
    plane_sem,
    out_sem,
    lat_send,
    lat_recv,
    lon_send,
    lon_recv,
    coef_send,
    coef_recv,
    part_send,
    part_recv,
    sum1_send,
    sum1_recv,
    sum2_send,
    sum2_recv,
):
    rows, cols = diff_hbm.shape
    tiles = cols // LANES
    ext_rows = rows + 2 * DEPTH
    i_lon, i_lat, i_rep = lax.axis_index("lon"), lax.axis_index("lat"), lax.axis_index("rep")

    def at(d_lon, d_lat):
        return (
            lax.rem(i_lon + n_lon + d_lon, n_lon),
            lax.rem(i_lat + n_lat + d_lat, n_lat),
            i_rep,
        )

    other = (i_lon, i_lat, 1 - i_rep)
    size1, size2 = n_lat, 2 * n_lon
    i_z, i_half = i_lat // 2, lax.rem(i_lat, 2)
    me1 = i_z * 2 + i_rep
    me2 = i_half * n_lon + i_lon

    def peer1(index):
        return (i_lon, (index // 2) * 2 + i_half, lax.rem(index, 2))

    def peer2(index):
        return (lax.rem(index, n_lon), i_z * 2 + index // n_lon, i_rep)

    neighbours = [(a, b) for a in (-1, 0, 1) for b in (-1, 0, 1) if (a, b) != (0, 0)]
    barrier = pltpu.get_barrier_semaphore()
    for a, b in neighbours:
        pl.semaphore_signal(barrier, inc=1, device_id=at(a, b), device_id_type=MESH)

    def greet(first, stop, peer, me, size):
        def one(k, carry):
            pl.semaphore_signal(
                barrier, inc=1, device_id=peer(lax.rem(me + k, size)), device_id_type=MESH
            )
            return carry

        lax.fori_loop(first, stop, one, 0)

    loads = [
        pltpu.make_async_copy(src, dst, load_sem.at[k])
        for k, (src, dst) in enumerate(
            (
                (diff_hbm, coef.at[0]),
                (ocean_hbm, ocean),
                (cell_hbm, cell),
                (weight_hbm, weight),
                (masks_hbm, masks),
                (phase_hbm, phase),
                (count_hbm, count),
            )
        )
    ]
    own = pl.ds(DEPTH, rows)
    planes = [
        pltpu.make_async_copy(
            planes_hbm.at[16 * rh + 2 * m + p], start.at[rh, p, own, m], plane_sem.at[rh, p, m]
        )
        for rh in range(GROUPS)
        for p in range(2)
        for m in range(8)
    ]
    for load in loads[:2] + planes + loads[5:] + loads[2:5]:
        load.start()
    greet(1, size1, peer1, me1, size1)
    greet(1, size2, peer2, me2, size2)

    lane = lax.broadcasted_iota(jnp.int32, (8, LANES), 1)
    sub = lax.broadcasted_iota(jnp.int32, (8, LANES), 0)
    loads[5].wait()
    angle = jnp.zeros((8, LANES), jnp.float32)
    for c in range(CONST):
        one = jnp.broadcast_to(phase[0:1, c : c + 1], (8, LANES))
        angle = jnp.where(lax.rem(sub, CONST) == c, one, angle)
    trig[0] = DAMPING * jnp.cos(angle)
    trig[1] = DAMPING * jnp.sin(angle)

    def turn(value, shift):
        shift %= LANES
        return pltpu.roll(value, shift, 1) if shift else value

    def span(t):
        return slice(t * LANES, (t + 1) * LANES)

    def set_factors(ext, t, diffusivity, wet):
        inverse = jnp.where(diffusivity > 0.0, 1.0 / jnp.where(diffusivity > 0.0, diffusivity, 1.0), 0.0)
        coupled = wet * diffusivity
        for i in range(8):
            d, w, v, u = (
                jnp.broadcast_to(x[i : i + 1], (8, LANES))
                for x in (diffusivity, wet, inverse, coupled)
            )
            sinus = w * trig[1]
            factor[0, ext + i, :, span(t)] = w * trig[0] - 4.0 * u
            factor[1, ext + i, :, span(t)] = sinus
            factor[2, ext + i, :, span(t)] = -sinus
            factor[3, ext + i, :, span(t)] = u
            factor[4, ext + i, :, span(t)] = v

    for load in loads[:2]:
        load.wait()
    coef[1] = ocean[...].astype(jnp.float32)
    for load in planes:
        load.wait()

    def prepare(block, carry):
        row = pl.multiple_of(block * 8, 8)
        for t in range(tiles):
            diffusivity = coef[0, pl.ds(row, 8), span(t)]
            for i in range(8):
                d = jnp.broadcast_to(diffusivity[i : i + 1], (8, LANES))
                for rh in range(GROUPS):
                    for p in range(2):
                        index = (rh, p, DEPTH + row + i, slice(None), span(t))
                        start[index] = d * start[index]
        return carry

    lax.fori_loop(0, rows // 8, prepare, 0)

    slot = lane // DEPTH

    def pack_half(rb, carry):
        row = rb * 16
        for g in range(2 * GROUPS + 1):
            to_west = jnp.zeros((8, LANES), jnp.float32)
            to_east = jnp.zeros((8, LANES), jnp.float32)
            for k in range(16 if g < 2 * GROUPS else 4):
                if g < 2 * GROUPS:
                    index = (g // 2, g % 2, DEPTH + row + k, slice(None))
                    left, right = start[index + (span(0),)], start[index + (span(tiles - 1),)]
                else:
                    some = pl.ds(pl.multiple_of(row + 8 * (k % 2), 8), 8)
                    left, right = coef[k // 2, some, span(0)], coef[k // 2, some, span(tiles - 1)]
                to_west = jnp.where(slot == k, turn(left, DEPTH * k), to_west)
                to_east = jnp.where(slot == k, turn(right, DEPTH * (k + 1)), to_east)
            pack[0, rb, g] = to_west
            pack[1, rb, g] = to_east
        return carry

    lax.fori_loop(0, 2, pack_half, 0)

    mains, strips = (start, odd, even), (strip_start, strip_odd, strip_even)

    def sweep(refs, prefix, step, ext, count, widths, offset):
        src = refs[0] if step == 1 else refs[1 + step % 2]
        dst = refs[1 if step % 2 else 2]
        sign = 1 if step <= SWEEPS else 2
        value = [
            [
                [src[(*prefix, p, ext + i, slice(None), span(t))] for t in range(widths)]
                for p in range(2)
            ]
            for i in range(-1, count + 1)
        ]
        for i in range(count):
            around = []
            for p in range(2):
                here = value[i + 1][p]
                right = [pltpu.roll(v, 1, 1) for v in here]
                left = [pltpu.roll(v, LANES - 1, 1) for v in here]
                for t in range(widths):
                    w, e = right[t], left[t]
                    if t > 0:
                        w = jnp.where(lane == 0, right[t - 1], w)
                    if t < widths - 1:
                        e = jnp.where(lane == LANES - 1, left[t + 1], e)
                    around.append((value[i][p][t] + value[i + 2][p][t]) + (w + e))
            for t in range(widths):
                at_row = (ext + i, slice(None), span(t + offset))
                a, s, u = factor[(0, *at_row)], factor[(sign, *at_row)], factor[(3, *at_row)]
                real, imag = value[i + 1][0][t], value[i + 1][1][t]
                results = [
                    (a * real + s * imag) + u * around[t],
                    (a * imag - s * real) + u * around[widths + t],
                ]
                if step == SWEEPS:
                    results = [factor[(4, *at_row)] * v for v in results]
                for p in range(2):
                    dst[(*prefix, p, ext + i, slice(None), span(t))] = results[p]

    def main_rows(rh, step, ext, count):
        sweep(mains, (rh,), step, ext, count, tiles, 0)

    def strip_rows(step, ext, count):
        sweep(strips, (), step, ext, count, 1, tiles)

    def interior(step, size, body):
        chunks = (rows - 2 * step + size - 1) // size

        def one(k, carry):
            body(DEPTH + jnp.minimum(step + size * k, rows - size - step))
            return carry

        lax.fori_loop(0, chunks, one, 0)

    def interior_main(steps):
        for step in steps:

            def both(ext, step=step):
                for rh in range(GROUPS):
                    main_rows(rh, step, ext, 8)

            interior(step, 8, both)

    def main_factors(block, carry):
        row = pl.multiple_of(block * 8, 8)
        for t in range(tiles):
            set_factors(
                DEPTH + row, t, coef[0, pl.ds(row, 8), span(t)], coef[1, pl.ds(row, 8), span(t)]
            )
        return carry

    lax.fori_loop(0, rows // 8, main_factors, 0)

    pl.semaphore_wait(barrier, len(neighbours) + size1 - 1 + size2 - 1)

    def send(src, dst, sends, recvs, index, device):
        copy = pltpu.make_async_remote_copy(
            src, dst, sends.at[index], recvs.at[index], device_id=device, device_id_type=MESH
        )
        copy.start()
        return copy

    first, last = pl.ds(DEPTH, DEPTH), pl.ds(rows, DEPTH)
    head, tail = pl.ds(0, DEPTH), pl.ds(rows + DEPTH, DEPTH)
    lon_copies = [
        send(pack.at[0], east.at[pl.ds(1, 2)], lon_send, lon_recv, 0, at(-1, 0)),
        send(pack.at[1], west.at[pl.ds(1, 2)], lon_send, lon_recv, 1, at(1, 0)),
    ]
    coef_copies = [
        send(coef.at[:, last_rows], coef_lat.at[side], coef_send, coef_recv, side, at(0, hop))
        for side, (last_rows, hop) in enumerate(
            ((pl.ds(rows - DEPTH, DEPTH), 1), (pl.ds(0, DEPTH), -1))
        )
    ]
    lat_copies = []
    for rh in range(GROUPS):
        if rh == 1:
            corner_copies = [
                send(pack.at[0, 1], east.at[0], lon_send, lon_recv, 2, at(-1, 1)),
                send(pack.at[0, 0], east.at[3], lon_send, lon_recv, 3, at(-1, -1)),
                send(pack.at[1, 1], west.at[0], lon_send, lon_recv, 4, at(1, 1)),
                send(pack.at[1, 0], west.at[3], lon_send, lon_recv, 5, at(1, -1)),
            ]
        lat_copies.append(
            [
                send(
                    start.at[rh, p, src],
                    start.at[rh, p, dst],
                    lat_send,
                    lat_recv,
                    4 * rh + 2 * p + side,
                    at(0, hop),
                )
                for p in range(2)
                for side, (src, dst, hop) in enumerate(((last, head, 1), (first, tail, -1)))
            ]
        )

    interior_main(range(1, DEPTH + 1))

    def strip_factors(block, main_of, valid):
        rb, half = (block + 1) // 2, (block + 1) % 2
        built = []
        for j in range(2):
            left, right = main_of(j, 0), main_of(j, tiles - 1)
            at_slot = DEPTH * (2 * j + half)
            value = jnp.where(lane < 48, turn(left, 32), 0.0)
            value = jnp.where(lane < 32, turn(west[rb, 2 * GROUPS], 24 - at_slot), value)
            value = jnp.where(lane < 24, turn(east[rb, 2 * GROUPS], 16 - at_slot), value)
            value = jnp.where(lane < 16, turn(right, 16), value)
            value = jnp.where(lane < 64, value, pltpu.roll(value, 64, 1))
            built.append(value if valid is None else jnp.where(valid, value, 0.0))
        set_factors(block * 8, tiles, *built)

    def strip_row(ext, rb, k, valid):
        for p in range(2):
            value = jnp.zeros((8, LANES), jnp.float32)
            for rh in range(GROUPS):
                base = 64 * rh
                index = (rh, p, ext, slice(None))
                part = jnp.where(lane < base + 48, turn(start[index + (span(0),)], base + 32), 0.0)
                part = jnp.where(
                    lane < base + 32, turn(west[rb, 2 * rh + p], base + 24 - DEPTH * k), part
                )
                part = jnp.where(
                    lane < base + 24, turn(east[rb, 2 * rh + p], base + 16 - DEPTH * k), part
                )
                part = jnp.where(
                    lane < base + 16, turn(start[index + (span(tiles - 1),)], base + 16), part
                )
                value = part if rh == 0 else jnp.where(lane < base, value, part)
            if valid is not None:
                value = jnp.where(valid, value, 0.0)
            strip_start[p, ext] = value

    def strip_body(rb, carry):
        for k in range(16):
            strip_row(DEPTH + rb * 16 + k, rb + 1, k, None)
        return carry

    loads[2].wait()
    loads[3].wait()
    loads[6].wait()
    live_slots = jnp.broadcast_to(count[...], (1, LANES))
    row_id = lax.broadcasted_iota(jnp.int32, (rows, LANES), 0)
    col_id = lax.broadcasted_iota(jnp.int32, (cols, LANES), 0)
    lane_1 = lax.broadcasted_iota(jnp.int32, (1, LANES), 1)

    def add_sites(j, total):
        cells = cell[pl.ds(j, 1), :]
        value = jnp.where(j * LANES + lane_1 < live_slots, weight[pl.ds(j, 1), :], 0.0)
        one = value.astype(jnp.bfloat16)
        rest = value - one.astype(jnp.float32)
        two = rest.astype(jnp.bfloat16)
        three = rest - two.astype(jnp.float32)
        hit_row = jnp.broadcast_to(cells // cols, (rows, LANES)) == row_id
        hit_col = jnp.broadcast_to(lax.rem(cells, cols), (cols, LANES)) == col_id
        terms = [
            jnp.where(hit_row, jnp.broadcast_to(term.astype(jnp.float32), (rows, LANES)), 0.0)
            for term in (one, two, three)
        ]
        lhs = jnp.concatenate(terms, axis=0).astype(jnp.bfloat16)
        rhs = jnp.where(hit_col, 1.0, 0.0).astype(jnp.bfloat16)
        return total + lax.dot_general(
            lhs, rhs, (((1,), (1,)), ((), ())), preferred_element_type=jnp.float32
        )

    summed = lax.fori_loop(
        0, cell.shape[0], add_sites, jnp.zeros((3 * rows, cols), jnp.float32)
    )
    summed = summed[:rows] + summed[rows : 2 * rows] + summed[2 * rows :]
    for row in range(rows):
        grid_w[row] = jnp.broadcast_to(summed[row : row + 1], (8, cols))

    for copy in lon_copies:
        copy.wait_recv()
    for block in range(1, 1 + rows // 8):
        strip_factors(
            block, lambda j, t, block=block: coef[j, pl.ds(8 * block - 8, 8), span(t)], None
        )
    lax.fori_loop(0, 2, strip_body, 0)
    for step in range(1, DEPTH + 1):
        interior(step, 16, lambda ext, step=step: strip_rows(step, ext, 16))

    def merge(first_row, length):
        for ext in range(DEPTH + first_row, DEPTH + first_row + length):
            for p in range(2):
                value = strip_even[p, ext]
                for rh in range(GROUPS):
                    left = even.at[rh, p, ext, :, span(0)]
                    right = even.at[rh, p, ext, :, span(tiles - 1)]
                    pltpu.store(left, turn(value, -32 - 64 * rh), mask=lane < DEPTH)
                    pltpu.store(
                        right, turn(value, LANES - 16 - 64 * rh), mask=lane >= LANES - DEPTH
                    )

    def share(rh, first_row, length, index):
        return send(
            even.at[rh, 1 - i_rep, pl.ds(DEPTH + first_row, length)],
            partner.at[rh, pl.ds(first_row, length)],
            part_send,
            part_recv,
            index,
            other,
        )

    merge(DEPTH, rows - 2 * DEPTH)
    parts = [share(rh, DEPTH, rows - 2 * DEPTH, rh) for rh in range(GROUPS)]

    acc[...] = jnp.zeros_like(acc)

    def own_rows(first_row, length):
        def one(block, totals):
            totals = list(totals)
            for row, p, t in [
                (first_row + 4 * block + i, p, t)
                for i in range(4)
                for p in range(2)
                for t in range(tiles)
            ]:
                values = [
                    even[rh, p, DEPTH + row, :, span(t)] for rh in range(GROUPS)
                ]
                scaled = [grid_w[row, :, span(t)] * v for v in values]
                turned = [pltpu.roll(v, 4, 0) for v in scaled]
                for j, (a, b) in enumerate(OWN_PAIRS):
                    totals[2 * j] += scaled[a] * values[b]
                    totals[2 * j + 1] += turned[a] * values[b]
            return tuple(totals)

        totals = lax.fori_loop(
            0, length // 4, one, tuple(acc[j] for j in range(6))
        )
        for j in range(6):
            acc[j] = totals[j]

    def cross_rows(first_row, length):
        def one(block, totals):
            totals = list(totals)
            for row, t in [
                (first_row + 4 * block + i, t) for i in range(4) for t in range(tiles)
            ]:
                scaled = [
                    grid_w[row, :, span(t)] * even[rh, i_rep, DEPTH + row, :, span(t)]
                    for rh in range(GROUPS)
                ]
                turned = [pltpu.roll(v, 4, 0) for v in scaled]
                values = [partner[rh, row, :, span(t)] for rh in range(GROUPS)]
                for j, (a, b) in enumerate(CROSS_PAIRS):
                    totals[2 * j] += scaled[a] * values[b]
                    totals[2 * j + 1] += turned[a] * values[b]
            return tuple(totals)

        totals = lax.fori_loop(
            0, length // 4, one, tuple(acc[6 + j] for j in range(8))
        )
        for j in range(8):
            acc[6 + j] = totals[j]

    own_rows(DEPTH, rows - 2 * DEPTH)
    for copy in parts:
        copy.wait_recv()
    cross_rows(DEPTH, rows - 2 * DEPTH)

    north_in, south_in = i_lat > 0, i_lat < n_lat - 1
    for copy in coef_copies:
        copy.wait_recv()
    for side, (block, valid) in enumerate(((0, north_in), (ext_rows // 8 - 1, south_in))):
        for t in range(tiles):
            set_factors(
                8 * block,
                t,
                *(jnp.where(valid, coef_lat[side, j, :, span(t)], 0.0) for j in range(2)),
            )
    for copy in corner_copies:
        copy.wait_recv()
    for side, (block, valid) in enumerate(((0, north_in), (ext_rows // 8 - 1, south_in))):
        strip_factors(block, lambda j, t, side=side: coef_lat[side, j, :, span(t)], valid)
    for some in lat_copies:
        for copy in some:
            copy.wait_recv()
    for rh in range(GROUPS):
        for ext, valid in ((DEPTH - 1, north_in), (rows + DEPTH, south_in)):
            for p in range(2):
                start[rh, p, ext] = jnp.where(valid, start[rh, p, ext], 0.0)
    for i in range(DEPTH):
        strip_row(i, 0, DEPTH + i, north_in)
        strip_row(rows + DEPTH + i, 3, i, south_in)
    for step in range(1, DEPTH + 1):
        for ext in (step, rows + DEPTH - step):
            for rh in range(GROUPS):
                main_rows(rh, step, ext, DEPTH)
            strip_rows(step, ext, DEPTH)
    merge(0, DEPTH)
    merge(rows - DEPTH, DEPTH)
    late = []
    for rh in range(GROUPS):
        late.append(share(rh, 0, DEPTH, 2 + 2 * rh))
        late.append(share(rh, rows - DEPTH, DEPTH, 3 + 2 * rh))
    stores = [
        pltpu.make_async_copy(
            even.at[rh, p, own, m], rep_out.at[16 * rh + 2 * m + p], out_sem.at[rh, p, m]
        )
        for rh in range(GROUPS)
        for p in range(2)
        for m in range(8)
    ]
    own_rows(0, DEPTH)
    own_rows(rows - DEPTH, DEPTH)
    for copy in late:
        copy.wait_recv()
    cross_rows(0, DEPTH)
    cross_rows(rows - DEPTH, DEPTH)

    packed = jnp.zeros((8, LANES), jnp.float32)
    for j in range(14):
        packed = jnp.where(lane == j, jnp.sum(acc[j], axis=1, keepdims=True), packed)
    packed = packed + pltpu.roll(packed, 7, 0)
    packed = packed + pltpu.roll(packed, 6, 0)
    second = pltpu.roll(pltpu.roll(packed, 4, 0), 16, 1)
    packed = jnp.where(lane < 16, packed, second)
    packed = jnp.where(i_rep == 0, packed, pltpu.roll(packed, 32, 1))

    def sum_start(row, buffer, me, size, peer, sends, recvs):
        buffer[me] = row
        for k in range(1, size):
            target = lax.rem(me + k, size)
            copy = pltpu.make_async_remote_copy(
                buffer.at[me],
                buffer.at[me],
                sends,
                recvs,
                device_id=peer(target),
                device_id_type=MESH,
            )
            copy.start()

    def sum_end(buffer, me, size, peer, sends, recvs):
        several = buffer.at[pl.ds(0, size - 1)]
        pltpu.make_async_remote_copy(
            several, several, sends, recvs, device_id=peer(me), device_id_type=MESH
        ).wait_recv()
        total = buffer[0]
        for k in range(1, size):
            total = total + buffer[k]
        return total

    def sum_sent(buffer, me, size, peer, sends, recvs):
        several = buffer.at[pl.ds(0, size - 1)]
        pltpu.make_async_remote_copy(
            several, several, sends, recvs, device_id=peer(me), device_id_type=MESH
        ).wait_send()

    first_sum = (stage1, me1, size1, peer1, sum1_send, sum1_recv)
    second_sum = (stage2, me2, size2, peer2, sum2_send, sum2_recv)
    sum_start(packed[0:1], *first_sum)
    for store in stores:
        store.start()
    for copy in lon_copies + coef_copies + corner_copies + parts + late:
        copy.wait_send()
    for some in lat_copies:
        for copy in some:
            copy.wait_send()
    loads[4].wait()
    row = sum_end(*first_sum)
    sum_start(row, *second_sum)
    sum_sent(*first_sum)
    for store in stores:
        store.wait()
    row = sum_end(*second_sum)

    row = jnp.broadcast_to(row, (8, LANES))
    result = jnp.zeros((8, LANES), jnp.float32)
    for q in range(8):
        result = jnp.where(
            lane == q, jnp.sum(row * masks[i_rep, q], axis=1, keepdims=True), result
        )
    gram_out[...] = result[0:4, 0:8]

    sum_sent(*second_sum)


def local(n_lon, n_lat, forcing, diffusivity, ocean, phase, site_cell, site_count, site_weight):
    reps, const, parts, rows, cols = forcing.shape
    planes = reps * const * parts
    slots = site_cell.shape[2]
    masks = jnp.asarray(entry_masks(float(n_lon * n_lat * slots)))
    ext = rows + 2 * DEPTH
    wide = cols + LANES
    any_space = pl.BlockSpec(memory_space=pl.ANY)
    vmem = pl.BlockSpec(memory_space=pltpu.VMEM)
    f32 = jnp.float32
    dma = pltpu.SemaphoreType.DMA
    size1, size2 = n_lat, 2 * n_lon
    representer, gram = pl.pallas_call(
        functools.partial(kernel, n_lon, n_lat),
        out_shape=(
            jax.ShapeDtypeStruct((planes, rows, cols), f32),
            jax.ShapeDtypeStruct((reps, 2 * reps), f32),
        ),
        in_specs=[any_space] * 8,
        out_specs=(any_space, vmem),
        scratch_shapes=[
            *[pltpu.VMEM((GROUPS, 2, ext, 8, cols), f32)] * 3,
            *[pltpu.VMEM((2, ext, 8, LANES), f32)] * 3,
            pltpu.VMEM((2, 2, 2 * GROUPS + 1, 8, LANES), f32),
            pltpu.VMEM((4, 2 * GROUPS + 1, 8, LANES), f32),
            pltpu.VMEM((4, 2 * GROUPS + 1, 8, LANES), f32),
            pltpu.VMEM((2, rows, cols), f32),
            pltpu.VMEM((rows, cols), jnp.int32),
            pltpu.VMEM((2, 2, DEPTH, cols), f32),
            pltpu.VMEM((5, ext, 8, wide), f32),
            pltpu.VMEM((2, 8, LANES), f32),
            pltpu.VMEM((slots // LANES, LANES), jnp.int32),
            pltpu.VMEM((slots // LANES, LANES), f32),
            pltpu.VMEM(masks.shape, f32),
            pltpu.VMEM((1, CONST), f32),
            pltpu.VMEM((1, 1), jnp.int32),
            pltpu.VMEM((rows, 8, cols), f32),
            pltpu.VMEM((GROUPS, rows, 8, cols), f32),
            pltpu.VMEM((14, 8, LANES), f32),
            pltpu.VMEM((size1, 1, LANES), f32),
            pltpu.VMEM((size2, 1, LANES), f32),
            dma((7,)),
            dma((GROUPS, 2, 8)),
            dma((GROUPS, 2, 8)),
            dma((8,)),
            dma((8,)),
            dma((6,)),
            dma((6,)),
            dma((2,)),
            dma((2,)),
            dma((6,)),
            dma((6,)),
            dma,
            dma,
            dma,
            dma,
        ],
        compiler_params=pltpu.CompilerParams(
            collective_id=0, has_side_effects=True, vmem_limit_bytes=67043328
        ),
        name="representer_block",
    )(
        forcing.reshape(planes, rows, cols),
        diffusivity,
        ocean,
        site_cell.reshape(slots // LANES, LANES),
        site_weight.reshape(slots // LANES, LANES),
        masks,
        phase.reshape(1, CONST),
        site_count,
    )
    return representer.reshape(forcing.shape), gram


def solution(mesh):
    return jax.shard_map(
        functools.partial(local, mesh.shape["lon"], mesh.shape["lat"]),
        mesh=mesh,
        in_specs=(
            P("rep", None, None, "lat", "lon"),
            P("lat", "lon"),
            P("lat", "lon"),
            P(),
            P("lat", "lon", None),
            P("lat", "lon"),
            P("lat", "lon", None),
        ),
        out_specs=(P("rep", None, None, "lat", "lon"), P("rep", None)),
        check_vma=False,
    )
```

```python
import functools

import jax
import jax.numpy as jnp
import numpy as np
from jax import lax
from jax.experimental import pallas as pl
from jax.experimental.pallas import tpu as pltpu
from jax.sharding import PartitionSpec as P

CONST = 4
SWEEPS = 4
DAMPING = 0.9
MESH = pl.DeviceIdType.MESH

DEPTH = 2 * SWEEPS
GROUPS = 2
LANES = 128
OWN_PAIRS = ((0, 0), (1, 1), (0, 1))
CROSS_PAIRS = ((0, 0), (0, 1), (1, 0), (1, 1))


def entry_lanes(rep, row, col):
    a, ra = divmod(row, 2)
    group, local = divmod(col, 4)
    b, rb = divmod(local, 2)
    if group == rep:
        if a > b:
            a, ra, b, rb = b, rb, a, ra
        at = OWN_PAIRS.index((a, b)) * 2 + (ra != rb)
        return [32 * rep + 16 * rb + at]
    first = 6 + CROSS_PAIRS.index((a, b)) * 2 + (ra != rb)
    second = 6 + CROSS_PAIRS.index((b, a)) * 2 + (ra != rb)
    return [32 * rep + 16 * rb + first, 32 * group + 16 * ra + second]


def entry_masks(scale):
    masks = np.zeros((2, 8, 8, LANES), np.float32)
    for rep in range(2):
        for row in range(4):
            for col in range(8):
                for lane in entry_lanes(rep, row, col):
                    masks[rep, col, row, lane] = 1.0 / scale
    return masks


def kernel(
    n_lon,
    n_lat,
    planes_hbm,
    diff_hbm,
    ocean_hbm,
    cell_hbm,
    weight_hbm,
    masks_hbm,
    phase_hbm,
    count_hbm,
    rep_out,
    gram_out,
    start,
    odd,
    even,
    strip_start,
    strip_odd,
    strip_even,
    pack,
    east,
    west,
    coef,
    ocean,
    coef_lat,
    factor,
    trig,
    cell,
    weight,
    masks,
    phase,
    count,
    grid_w,
    partner,
    acc,
    stage1,
    stage2,
    ready,
    load_sem,
    plane_sem,
    out_sem,
    lat_send,
    lat_recv,
    lon_send,
    lon_recv,
    coef_send,
    coef_recv,
    part_send,
    part_recv,
    sum1_send,
    sum1_recv,
    sum2_send,
    sum2_recv,
):
    rows, cols = diff_hbm.shape
    tiles = cols // LANES
    ext_rows = rows + 2 * DEPTH
    i_lon, i_lat, i_rep = lax.axis_index("lon"), lax.axis_index("lat"), lax.axis_index("rep")

    def at(d_lon, d_lat):
        return (
            lax.rem(i_lon + n_lon + d_lon, n_lon),
            lax.rem(i_lat + n_lat + d_lat, n_lat),
            i_rep,
        )

    other = (i_lon, i_lat, 1 - i_rep)
    size1, size2 = n_lat, 2 * n_lon
    i_z, i_half = i_lat // 2, lax.rem(i_lat, 2)
    me1 = i_z * 2 + i_rep
    me2 = i_half * n_lon + i_lon

    def peer1(index):
        return (i_lon, (index // 2) * 2 + i_half, lax.rem(index, 2))

    def peer2(index):
        return (lax.rem(index, n_lon), i_z * 2 + index // n_lon, i_rep)

    def by_distance(length):
        return sorted(range(length), key=lambda k: -min(k, length - k))

    others1 = [
        lax.rem(i_z + z, size1 // 2) * 2 + lax.rem(i_rep + c, 2)
        for z in by_distance(size1 // 2)
        for c in (1, 0)
        if (z, c) != (0, 0)
    ]
    others2 = [
        lax.rem(i_half + h, 2) * n_lon + lax.rem(i_lon + l, n_lon)
        for l in by_distance(n_lon)
        for h in (1, 0)
        if (h, l) != (0, 0)
    ]

    sides = [at(1, 0), at(-1, 0), at(0, 1), at(0, -1)]
    known = (
        sides,
        [at(2, 0), at(-2, 0), at(0, 2), at(0, -2)],
        [at(0, 4), at(0, -4), at(0, 1), at(0, -1)],
        [other],
    )
    barrier = pltpu.get_barrier_semaphore()
    for device in sides + [other]:
        pl.semaphore_signal(barrier, inc=1, device_id=device, device_id_type=MESH)

    def tell(level):
        for device in known[level]:
            pl.semaphore_signal(ready.at[level], inc=1, device_id=device, device_id_type=MESH)

    def learn(level):
        pl.semaphore_wait(ready.at[level], len(known[level]))

    loads = [
        pltpu.make_async_copy(src, dst, load_sem.at[k])
        for k, (src, dst) in enumerate(
            (
                (diff_hbm, coef.at[0]),
                (ocean_hbm, ocean),
                (cell_hbm, cell),
                (weight_hbm, weight),
                (masks_hbm, masks),
                (phase_hbm, phase),
                (count_hbm, count),
            )
        )
    ]
    own = pl.ds(DEPTH, rows)
    planes = [
        pltpu.make_async_copy(
            planes_hbm.at[16 * rh + 2 * m + p], start.at[rh, p, own, m], plane_sem.at[rh, p, m]
        )
        for rh in range(GROUPS)
        for p in range(2)
        for m in range(8)
    ]
    for load in loads[:2] + planes + loads[5:] + loads[2:5]:
        load.start()

    lane = lax.broadcasted_iota(jnp.int32, (8, LANES), 1)
    sub = lax.broadcasted_iota(jnp.int32, (8, LANES), 0)
    loads[5].wait()
    angle = jnp.zeros((8, LANES), jnp.float32)
    for c in range(CONST):
        one = jnp.broadcast_to(phase[0:1, c : c + 1], (8, LANES))
        angle = jnp.where(lax.rem(sub, CONST) == c, one, angle)
    trig[0] = DAMPING * jnp.cos(angle)
    trig[1] = DAMPING * jnp.sin(angle)

    def turn(value, shift):
        shift %= LANES
        return pltpu.roll(value, shift, 1) if shift else value

    def span(t):
        return slice(t * LANES, (t + 1) * LANES)

    def set_factors(ext, t, diffusivity, wet):
        inverse = jnp.where(diffusivity > 0.0, 1.0 / jnp.where(diffusivity > 0.0, diffusivity, 1.0), 0.0)
        coupled = wet * diffusivity
        for i in range(8):
            d, w, v, u = (
                jnp.broadcast_to(x[i : i + 1], (8, LANES))
                for x in (diffusivity, wet, inverse, coupled)
            )
            sinus = w * trig[1]
            factor[0, ext + i, :, span(t)] = w * trig[0] - 4.0 * u
            factor[1, ext + i, :, span(t)] = sinus
            factor[2, ext + i, :, span(t)] = -sinus
            factor[3, ext + i, :, span(t)] = u
            factor[4, ext + i, :, span(t)] = v

    for load in loads[:2]:
        load.wait()
    coef[1] = ocean[...].astype(jnp.float32)
    for load in planes:
        load.wait()

    def prepare(block, carry):
        row = pl.multiple_of(block * 8, 8)
        for t in range(tiles):
            diffusivity = coef[0, pl.ds(row, 8), span(t)]
            for i in range(8):
                d = jnp.broadcast_to(diffusivity[i : i + 1], (8, LANES))
                for rh in range(GROUPS):
                    for p in range(2):
                        index = (rh, p, DEPTH + row + i, slice(None), span(t))
                        start[index] = d * start[index]
        return carry

    lax.fori_loop(0, rows // 8, prepare, 0)

    slot = lane // DEPTH

    def pack_half(rb, carry):
        row = rb * 16
        for g in range(2 * GROUPS + 1):
            to_west = jnp.zeros((8, LANES), jnp.float32)
            to_east = jnp.zeros((8, LANES), jnp.float32)
            for k in range(16 if g < 2 * GROUPS else 4):
                if g < 2 * GROUPS:
                    index = (g // 2, g % 2, DEPTH + row + k, slice(None))
                    left, right = start[index + (span(0),)], start[index + (span(tiles - 1),)]
                else:
                    some = pl.ds(pl.multiple_of(row + 8 * (k % 2), 8), 8)
                    left, right = coef[k // 2, some, span(0)], coef[k // 2, some, span(tiles - 1)]
                to_west = jnp.where(slot == k, turn(left, DEPTH * k), to_west)
                to_east = jnp.where(slot == k, turn(right, DEPTH * (k + 1)), to_east)
            pack[0, rb, g] = to_west
            pack[1, rb, g] = to_east
        return carry

    lax.fori_loop(0, 2, pack_half, 0)

    mains, strips = (start, odd, even), (strip_start, strip_odd, strip_even)

    def sweep(refs, prefix, step, ext, count, widths, offset):
        src = refs[0] if step == 1 else refs[1 + step % 2]
        dst = refs[1 if step % 2 else 2]
        sign = 1 if step <= SWEEPS else 2
        value = [
            [
                [src[(*prefix, p, ext + i, slice(None), span(t))] for t in range(widths)]
                for p in range(2)
            ]
            for i in range(-1, count + 1)
        ]
        for i in range(count):
            around = []
            for p in range(2):
                here = value[i + 1][p]
                right = [pltpu.roll(v, 1, 1) for v in here]
                left = [pltpu.roll(v, LANES - 1, 1) for v in here]
                for t in range(widths):
                    w, e = right[t], left[t]
                    if t > 0:
                        w = jnp.where(lane == 0, right[t - 1], w)
                    if t < widths - 1:
                        e = jnp.where(lane == LANES - 1, left[t + 1], e)
                    around.append((value[i][p][t] + value[i + 2][p][t]) + (w + e))
            for t in range(widths):
                at_row = (ext + i, slice(None), span(t + offset))
                a, s, u = factor[(0, *at_row)], factor[(sign, *at_row)], factor[(3, *at_row)]
                real, imag = value[i + 1][0][t], value[i + 1][1][t]
                results = [
                    (a * real + s * imag) + u * around[t],
                    (a * imag - s * real) + u * around[widths + t],
                ]
                if step == SWEEPS:
                    results = [factor[(4, *at_row)] * v for v in results]
                for p in range(2):
                    dst[(*prefix, p, ext + i, slice(None), span(t))] = results[p]

    def main_rows(rh, step, ext, count):
        sweep(mains, (rh,), step, ext, count, tiles, 0)

    def strip_rows(step, ext, count):
        sweep(strips, (), step, ext, count, 1, tiles)

    def interior(step, size, body):
        chunks = (rows - 2 * step + size - 1) // size

        def one(k, carry):
            body(DEPTH + jnp.minimum(step + size * k, rows - size - step))
            return carry

        lax.fori_loop(0, chunks, one, 0)

    def interior_main(steps):
        for step in steps:

            def both(ext, step=step):
                for rh in range(GROUPS):
                    main_rows(rh, step, ext, 8)

            interior(step, 8, both)

    def main_factors(block, carry):
        row = pl.multiple_of(block * 8, 8)
        for t in range(tiles):
            set_factors(
                DEPTH + row, t, coef[0, pl.ds(row, 8), span(t)], coef[1, pl.ds(row, 8), span(t)]
            )
        return carry

    lax.fori_loop(0, rows // 8, main_factors, 0)

    pl.semaphore_wait(barrier, len(sides) + 1)
    tell(0)

    def send(src, dst, sends, recvs, index, device):
        copy = pltpu.make_async_remote_copy(
            src, dst, sends.at[index], recvs.at[index], device_id=device, device_id_type=MESH
        )
        copy.start()
        return copy

    first, last = pl.ds(DEPTH, DEPTH), pl.ds(rows, DEPTH)
    head, tail = pl.ds(0, DEPTH), pl.ds(rows + DEPTH, DEPTH)
    lon_copies = [
        send(pack.at[0], east.at[pl.ds(1, 2)], lon_send, lon_recv, 0, at(-1, 0)),
        send(pack.at[1], west.at[pl.ds(1, 2)], lon_send, lon_recv, 1, at(1, 0)),
    ]
    coef_copies = [
        send(coef.at[:, last_rows], coef_lat.at[side], coef_send, coef_recv, side, at(0, hop))
        for side, (last_rows, hop) in enumerate(
            ((pl.ds(rows - DEPTH, DEPTH), 1), (pl.ds(0, DEPTH), -1))
        )
    ]
    lat_copies = []
    for rh in range(GROUPS):
        lat_copies.append(
            [
                send(
                    start.at[rh, p, src],
                    start.at[rh, p, dst],
                    lat_send,
                    lat_recv,
                    4 * rh + 2 * p + side,
                    at(0, hop),
                )
                for p in range(2)
                for side, (src, dst, hop) in enumerate(((last, head, 1), (first, tail, -1)))
            ]
        )

    interior_main(range(1, SWEEPS + 1))
    learn(0)
    corner_copies = [
        send(pack.at[0, 1], east.at[0], lon_send, lon_recv, 2, at(-1, 1)),
        send(pack.at[0, 0], east.at[3], lon_send, lon_recv, 3, at(-1, -1)),
        send(pack.at[1, 1], west.at[0], lon_send, lon_recv, 4, at(1, 1)),
        send(pack.at[1, 0], west.at[3], lon_send, lon_recv, 5, at(1, -1)),
    ]
    tell(1)
    interior_main(range(SWEEPS + 1, DEPTH + 1))
    learn(1)
    tell(2)

    def strip_factors(block, main_of, valid):
        rb, half = (block + 1) // 2, (block + 1) % 2
        built = []
        for j in range(2):
            left, right = main_of(j, 0), main_of(j, tiles - 1)
            at_slot = DEPTH * (2 * j + half)
            value = jnp.where(lane < 48, turn(left, 32), 0.0)
            value = jnp.where(lane < 32, turn(west[rb, 2 * GROUPS], 24 - at_slot), value)
            value = jnp.where(lane < 24, turn(east[rb, 2 * GROUPS], 16 - at_slot), value)
            value = jnp.where(lane < 16, turn(right, 16), value)
            value = jnp.where(lane < 64, value, pltpu.roll(value, 64, 1))
            built.append(value if valid is None else jnp.where(valid, value, 0.0))
        set_factors(block * 8, tiles, *built)

    def strip_row(ext, rb, k, valid):
        for p in range(2):
            value = jnp.zeros((8, LANES), jnp.float32)
            for rh in range(GROUPS):
                base = 64 * rh
                index = (rh, p, ext, slice(None))
                part = jnp.where(lane < base + 48, turn(start[index + (span(0),)], base + 32), 0.0)
                part = jnp.where(
                    lane < base + 32, turn(west[rb, 2 * rh + p], base + 24 - DEPTH * k), part
                )
                part = jnp.where(
                    lane < base + 24, turn(east[rb, 2 * rh + p], base + 16 - DEPTH * k), part
                )
                part = jnp.where(
                    lane < base + 16, turn(start[index + (span(tiles - 1),)], base + 16), part
                )
                value = part if rh == 0 else jnp.where(lane < base, value, part)
            if valid is not None:
                value = jnp.where(valid, value, 0.0)
            strip_start[p, ext] = value

    def strip_body(rb, carry):
        for k in range(16):
            strip_row(DEPTH + rb * 16 + k, rb + 1, k, None)
        return carry

    loads[2].wait()
    loads[3].wait()
    loads[6].wait()
    live_slots = jnp.broadcast_to(count[...], (1, LANES))
    row_id = lax.broadcasted_iota(jnp.int32, (rows, LANES), 0)
    col_id = lax.broadcasted_iota(jnp.int32, (cols, LANES), 0)
    lane_1 = lax.broadcasted_iota(jnp.int32, (1, LANES), 1)

    def add_sites(j, total):
        cells = cell[pl.ds(j, 1), :]
        value = jnp.where(j * LANES + lane_1 < live_slots, weight[pl.ds(j, 1), :], 0.0)
        one = value.astype(jnp.bfloat16)
        rest = value - one.astype(jnp.float32)
        two = rest.astype(jnp.bfloat16)
        three = rest - two.astype(jnp.float32)
        hit_row = jnp.broadcast_to(cells // cols, (rows, LANES)) == row_id
        hit_col = jnp.broadcast_to(lax.rem(cells, cols), (cols, LANES)) == col_id
        terms = [
            jnp.where(hit_row, jnp.broadcast_to(term.astype(jnp.float32), (rows, LANES)), 0.0)
            for term in (one, two, three)
        ]
        lhs = jnp.concatenate(terms, axis=0).astype(jnp.bfloat16)
        rhs = jnp.where(hit_col, 1.0, 0.0).astype(jnp.bfloat16)
        return total + lax.dot_general(
            lhs, rhs, (((1,), (1,)), ((), ())), preferred_element_type=jnp.float32
        )

    summed = lax.fori_loop(
        0, cell.shape[0], add_sites, jnp.zeros((3 * rows, cols), jnp.float32)
    )
    summed = summed[:rows] + summed[rows : 2 * rows] + summed[2 * rows :]
    for row in range(rows):
        grid_w[row] = jnp.broadcast_to(summed[row : row + 1], (8, cols))

    for copy in lon_copies:
        copy.wait_recv()
    for block in range(1, 1 + rows // 8):
        strip_factors(
            block, lambda j, t, block=block: coef[j, pl.ds(8 * block - 8, 8), span(t)], None
        )
    lax.fori_loop(0, 2, strip_body, 0)
    for step in range(1, DEPTH + 1):
        interior(step, 16, lambda ext, step=step: strip_rows(step, ext, 16))

    def merge(first_row, length):
        for ext in range(DEPTH + first_row, DEPTH + first_row + length):
            for p in range(2):
                value = strip_even[p, ext]
                for rh in range(GROUPS):
                    left = even.at[rh, p, ext, :, span(0)]
                    right = even.at[rh, p, ext, :, span(tiles - 1)]
                    pltpu.store(left, turn(value, -32 - 64 * rh), mask=lane < DEPTH)
                    pltpu.store(
                        right, turn(value, LANES - 16 - 64 * rh), mask=lane >= LANES - DEPTH
                    )

    def share(rh, first_row, length, index):
        return send(
            even.at[rh, 1 - i_rep, pl.ds(DEPTH + first_row, length)],
            partner.at[rh, pl.ds(first_row, length)],
            part_send,
            part_recv,
            index,
            other,
        )

    merge(DEPTH, rows - 2 * DEPTH)
    parts = [share(rh, DEPTH, rows - 2 * DEPTH, rh) for rh in range(GROUPS)]

    learn(2)
    tell(3)
    acc[...] = jnp.zeros_like(acc)

    def own_rows(first_row, length):
        def one(block, totals):
            totals = list(totals)
            for row, p, t in [
                (first_row + 4 * block + i, p, t)
                for i in range(4)
                for p in range(2)
                for t in range(tiles)
            ]:
                values = [
                    even[rh, p, DEPTH + row, :, span(t)] for rh in range(GROUPS)
                ]
                scaled = [grid_w[row, :, span(t)] * v for v in values]
                turned = [pltpu.roll(v, 4, 0) for v in scaled]
                for j, (a, b) in enumerate(OWN_PAIRS):
                    totals[2 * j] += scaled[a] * values[b]
                    totals[2 * j + 1] += turned[a] * values[b]
            return tuple(totals)

        totals = lax.fori_loop(
            0, length // 4, one, tuple(acc[j] for j in range(6))
        )
        for j in range(6):
            acc[j] = totals[j]

    def cross_rows(first_row, length):
        def one(block, totals):
            totals = list(totals)
            for row, t in [
                (first_row + 4 * block + i, t) for i in range(4) for t in range(tiles)
            ]:
                scaled = [
                    grid_w[row, :, span(t)] * even[rh, i_rep, DEPTH + row, :, span(t)]
                    for rh in range(GROUPS)
                ]
                turned = [pltpu.roll(v, 4, 0) for v in scaled]
                values = [partner[rh, row, :, span(t)] for rh in range(GROUPS)]
                for j, (a, b) in enumerate(CROSS_PAIRS):
                    totals[2 * j] += scaled[a] * values[b]
                    totals[2 * j + 1] += turned[a] * values[b]
            return tuple(totals)

        totals = lax.fori_loop(
            0, length // 4, one, tuple(acc[6 + j] for j in range(8))
        )
        for j in range(8):
            acc[6 + j] = totals[j]

    own_rows(DEPTH, rows - 2 * DEPTH)
    for copy in parts:
        copy.wait_recv()
    cross_rows(DEPTH, rows - 2 * DEPTH)

    learn(3)
    north_in, south_in = i_lat > 0, i_lat < n_lat - 1
    for copy in coef_copies:
        copy.wait_recv()
    for side, (block, valid) in enumerate(((0, north_in), (ext_rows // 8 - 1, south_in))):
        for t in range(tiles):
            set_factors(
                8 * block,
                t,
                *(jnp.where(valid, coef_lat[side, j, :, span(t)], 0.0) for j in range(2)),
            )
    for copy in corner_copies:
        copy.wait_recv()
    for side, (block, valid) in enumerate(((0, north_in), (ext_rows // 8 - 1, south_in))):
        strip_factors(block, lambda j, t, side=side: coef_lat[side, j, :, span(t)], valid)
    for rh in range(GROUPS):
        for copy in lat_copies[rh]:
            copy.wait_recv()
        for ext, valid in ((DEPTH - 1, north_in), (rows + DEPTH, south_in)):
            for p in range(2):
                start[rh, p, ext] = jnp.where(valid, start[rh, p, ext], 0.0)
        if rh == GROUPS - 1:
            for i in range(DEPTH):
                strip_row(i, 0, DEPTH + i, north_in)
                strip_row(rows + DEPTH + i, 3, i, south_in)
        for step in range(1, DEPTH + 1):
            for ext in (step, rows + DEPTH - step):
                main_rows(rh, step, ext, DEPTH)
                if rh == GROUPS - 1:
                    strip_rows(step, ext, DEPTH)
    merge(0, DEPTH)
    merge(rows - DEPTH, DEPTH)
    late = []
    for rh in range(GROUPS):
        late.append(share(rh, 0, DEPTH, 2 + 2 * rh))
        late.append(share(rh, rows - DEPTH, DEPTH, 3 + 2 * rh))
    stores = [
        pltpu.make_async_copy(
            even.at[rh, p, own, m], rep_out.at[16 * rh + 2 * m + p], out_sem.at[rh, p, m]
        )
        for rh in range(GROUPS)
        for p in range(2)
        for m in range(8)
    ]
    own_rows(0, DEPTH)
    own_rows(rows - DEPTH, DEPTH)
    for copy in late:
        copy.wait_recv()
    cross_rows(0, DEPTH)
    cross_rows(rows - DEPTH, DEPTH)

    packed = jnp.zeros((8, LANES), jnp.float32)
    for j in range(14):
        packed = jnp.where(lane == j, jnp.sum(acc[j], axis=1, keepdims=True), packed)
    packed = packed + pltpu.roll(packed, 7, 0)
    packed = packed + pltpu.roll(packed, 6, 0)
    second = pltpu.roll(pltpu.roll(packed, 4, 0), 16, 1)
    packed = jnp.where(lane < 16, packed, second)
    packed = jnp.where(i_rep == 0, packed, pltpu.roll(packed, 32, 1))

    def sum_start(row, buffer, me, size, peer, targets, sends, recvs):
        buffer[me] = row
        for target in targets:
            copy = pltpu.make_async_remote_copy(
                buffer.at[me],
                buffer.at[me],
                sends,
                recvs,
                device_id=peer(target),
                device_id_type=MESH,
            )
            copy.start()

    def sum_end(buffer, me, size, peer, targets, sends, recvs):
        several = buffer.at[pl.ds(0, size - 1)]
        pltpu.make_async_remote_copy(
            several, several, sends, recvs, device_id=peer(targets[0]), device_id_type=MESH
        ).wait_recv()
        total = buffer[0]
        for k in range(1, size):
            total = total + buffer[k]
        return total

    def sum_sent(buffer, me, size, peer, targets, sends, recvs):
        several = buffer.at[pl.ds(0, size - 1)]
        pltpu.make_async_remote_copy(
            several, several, sends, recvs, device_id=peer(targets[0]), device_id_type=MESH
        ).wait_send()

    first_sum = (stage1, me1, size1, peer1, others1, sum1_send, sum1_recv)
    second_sum = (stage2, me2, size2, peer2, others2, sum2_send, sum2_recv)
    sum_start(packed[0:1], *first_sum)
    for store in stores:
        store.start()
    for copy in lon_copies + coef_copies + corner_copies + parts + late:
        copy.wait_send()
    for some in lat_copies:
        for copy in some:
            copy.wait_send()
    loads[4].wait()
    row = sum_end(*first_sum)
    sum_start(row, *second_sum)
    sum_sent(*first_sum)
    for store in stores:
        store.wait()
    row = sum_end(*second_sum)

    row = jnp.broadcast_to(row, (8, LANES))
    result = jnp.zeros((8, LANES), jnp.float32)
    for q in range(8):
        result = jnp.where(
            lane == q, jnp.sum(row * masks[i_rep, q], axis=1, keepdims=True), result
        )
    gram_out[...] = result[0:4, 0:8]

    sum_sent(*second_sum)


def local(n_lon, n_lat, forcing, diffusivity, ocean, phase, site_cell, site_count, site_weight):
    reps, const, parts, rows, cols = forcing.shape
    planes = reps * const * parts
    slots = site_cell.shape[2]
    masks = jnp.asarray(entry_masks(float(n_lon * n_lat * slots)))
    ext = rows + 2 * DEPTH
    wide = cols + LANES
    any_space = pl.BlockSpec(memory_space=pl.ANY)
    vmem = pl.BlockSpec(memory_space=pltpu.VMEM)
    f32 = jnp.float32
    dma = pltpu.SemaphoreType.DMA
    size1, size2 = n_lat, 2 * n_lon
    representer, gram = pl.pallas_call(
        functools.partial(kernel, n_lon, n_lat),
        out_shape=(
            jax.ShapeDtypeStruct((planes, rows, cols), f32),
            jax.ShapeDtypeStruct((reps, 2 * reps), f32),
        ),
        in_specs=[any_space] * 8,
        out_specs=(any_space, vmem),
        scratch_shapes=[
            *[pltpu.VMEM((GROUPS, 2, ext, 8, cols), f32)] * 3,
            *[pltpu.VMEM((2, ext, 8, LANES), f32)] * 3,
            pltpu.VMEM((2, 2, 2 * GROUPS + 1, 8, LANES), f32),
            pltpu.VMEM((4, 2 * GROUPS + 1, 8, LANES), f32),
            pltpu.VMEM((4, 2 * GROUPS + 1, 8, LANES), f32),
            pltpu.VMEM((2, rows, cols), f32),
            pltpu.VMEM((rows, cols), jnp.int32),
            pltpu.VMEM((2, 2, DEPTH, cols), f32),
            pltpu.VMEM((5, ext, 8, wide), f32),
            pltpu.VMEM((2, 8, LANES), f32),
            pltpu.VMEM((slots // LANES, LANES), jnp.int32),
            pltpu.VMEM((slots // LANES, LANES), f32),
            pltpu.VMEM(masks.shape, f32),
            pltpu.VMEM((1, CONST), f32),
            pltpu.VMEM((1, 1), jnp.int32),
            pltpu.VMEM((rows, 8, cols), f32),
            pltpu.VMEM((GROUPS, rows, 8, cols), f32),
            pltpu.VMEM((14, 8, LANES), f32),
            pltpu.VMEM((size1, 1, LANES), f32),
            pltpu.VMEM((size2, 1, LANES), f32),
            pltpu.SemaphoreType.REGULAR((4,)),
            dma((7,)),
            dma((GROUPS, 2, 8)),
            dma((GROUPS, 2, 8)),
            dma((8,)),
            dma((8,)),
            dma((6,)),
            dma((6,)),
            dma((2,)),
            dma((2,)),
            dma((6,)),
            dma((6,)),
            dma,
            dma,
            dma,
            dma,
        ],
        compiler_params=pltpu.CompilerParams(
            collective_id=0, has_side_effects=True, vmem_limit_bytes=40 << 20
        ),
        name="representer_block",
    )(
        *[
            pltpu.with_memory_space_constraint(x, pltpu.HBM)
            for x in (
                forcing.reshape(planes, rows, cols),
                diffusivity,
                ocean,
                site_cell.reshape(slots // LANES, LANES),
                site_weight.reshape(slots // LANES, LANES),
                masks,
                phase.reshape(1, CONST),
            )
        ],
        site_count,
    )
    return representer.reshape(forcing.shape), gram


def solution(mesh):
    return jax.shard_map(
        functools.partial(local, mesh.shape["lon"], mesh.shape["lat"]),
        mesh=mesh,
        in_specs=(
            P("rep", None, None, "lat", "lon"),
            P("lat", "lon"),
            P("lat", "lon"),
            P(),
            P("lat", "lon", None),
            P("lat", "lon"),
            P("lat", "lon", None),
        ),
        out_specs=(P("rep", None, None, "lat", "lon"), P("rep", None)),
        check_vma=False,
    )
```

```python
import functools

import jax
import jax.numpy as jnp
import numpy as np
from jax import lax
from jax.experimental import pallas as pl
from jax.experimental.pallas import tpu as pltpu
from jax.sharding import PartitionSpec as P

CONST = 4
SWEEPS = 4
DAMPING = 0.9
MESH = pl.DeviceIdType.MESH

DEPTH = 2 * SWEEPS
GROUPS = 2
LANES = 128
OWN_PAIRS = ((0, 0), (1, 1), (0, 1))
CROSS_PAIRS = ((0, 0), (0, 1), (1, 0), (1, 1))


def entry_lanes(rep, row, col):
    a, ra = divmod(row, 2)
    group, local = divmod(col, 4)
    b, rb = divmod(local, 2)
    if group == rep:
        if a > b:
            a, ra, b, rb = b, rb, a, ra
        at = OWN_PAIRS.index((a, b)) * 2 + (ra != rb)
        return [32 * rep + 16 * rb + at]
    first = 6 + CROSS_PAIRS.index((a, b)) * 2 + (ra != rb)
    second = 6 + CROSS_PAIRS.index((b, a)) * 2 + (ra != rb)
    return [32 * rep + 16 * rb + first, 32 * group + 16 * ra + second]


def entry_masks(scale):
    masks = np.zeros((2, 8, 8, LANES), np.float32)
    for rep in range(2):
        for row in range(4):
            for col in range(8):
                for lane in entry_lanes(rep, row, col):
                    masks[rep, col, row, lane] = 1.0 / scale
    return masks


def kernel(
    n_lon,
    n_lat,
    planes_hbm,
    diff_hbm,
    ocean_hbm,
    cell_hbm,
    weight_hbm,
    masks_hbm,
    phase_hbm,
    count_hbm,
    rep_out,
    gram_out,
    start,
    odd,
    even,
    strip_start,
    strip_odd,
    strip_even,
    pack,
    east,
    west,
    coef,
    ocean,
    coef_lat,
    factor,
    trig,
    cell,
    weight,
    masks,
    phase,
    count,
    grid_w,
    partner,
    acc,
    stage1,
    stage2,
    ready,
    load_sem,
    plane_sem,
    out_sem,
    lat_send,
    lat_recv,
    lon_send,
    lon_recv,
    coef_send,
    coef_recv,
    part_send,
    part_recv,
    sum1_send,
    sum1_recv,
    sum2_send,
    sum2_recv,
):
    rows, cols = diff_hbm.shape
    tiles = cols // LANES
    ext_rows = rows + 2 * DEPTH
    i_lon, i_lat, i_rep = lax.axis_index("lon"), lax.axis_index("lat"), lax.axis_index("rep")

    def at(d_lon, d_lat):
        return (
            lax.rem(i_lon + n_lon + d_lon, n_lon),
            lax.rem(i_lat + n_lat + d_lat, n_lat),
            i_rep,
        )

    other = (i_lon, i_lat, 1 - i_rep)
    size1, size2 = n_lat, 2 * n_lon
    i_z, i_half = i_lat // 2, lax.rem(i_lat, 2)
    me1 = i_z * 2 + i_rep
    me2 = i_half * n_lon + i_lon

    def peer1(index):
        return (i_lon, (index // 2) * 2 + i_half, lax.rem(index, 2))

    def peer2(index):
        return (lax.rem(index, n_lon), i_z * 2 + index // n_lon, i_rep)

    def by_distance(length):
        return sorted(range(length), key=lambda k: -min(k, length - k))

    others1 = [
        lax.rem(i_z + z, size1 // 2) * 2 + lax.rem(i_rep + c, 2)
        for z in by_distance(size1 // 2)
        for c in (1, 0)
        if (z, c) != (0, 0)
    ]
    others2 = [
        lax.rem(i_half + h, 2) * n_lon + lax.rem(i_lon + l, n_lon)
        for l in by_distance(n_lon)
        for h in (1, 0)
        if (h, l) != (0, 0)
    ]

    sides = [at(1, 0), at(-1, 0), at(0, 1), at(0, -1)]
    known = (
        sides,
        [at(2, 0), at(-2, 0), at(0, 2), at(0, -2)],
        [at(0, 4), at(0, -4), at(0, 1), at(0, -1)],
        [other],
    )
    barrier = pltpu.get_barrier_semaphore()
    for device in sides + [other]:
        pl.semaphore_signal(barrier, inc=1, device_id=device, device_id_type=MESH)

    def tell(level):
        for device in known[level]:
            pl.semaphore_signal(ready.at[level], inc=1, device_id=device, device_id_type=MESH)

    def learn(level):
        pl.semaphore_wait(ready.at[level], len(known[level]))

    loads = [
        pltpu.make_async_copy(src, dst, load_sem.at[k])
        for k, (src, dst) in enumerate(
            (
                (diff_hbm, coef.at[0]),
                (ocean_hbm, ocean),
                (cell_hbm, cell),
                (weight_hbm, weight),
                (masks_hbm, masks),
                (phase_hbm, phase),
                (count_hbm, count),
            )
        )
    ]
    own = pl.ds(DEPTH, rows)
    planes = [
        pltpu.make_async_copy(
            planes_hbm.at[16 * rh + 2 * m + p], start.at[rh, p, own, m], plane_sem.at[rh, p, m]
        )
        for rh in range(GROUPS)
        for p in range(2)
        for m in range(8)
    ]
    for load in planes + loads[:2] + loads[5:] + loads[2:5]:
        load.start()

    lane = lax.broadcasted_iota(jnp.int32, (8, LANES), 1)
    sub = lax.broadcasted_iota(jnp.int32, (8, LANES), 0)
    loads[5].wait()
    angle = jnp.zeros((8, LANES), jnp.float32)
    for c in range(CONST):
        one = jnp.broadcast_to(phase[0:1, c : c + 1], (8, LANES))
        angle = jnp.where(lax.rem(sub, CONST) == c, one, angle)
    trig[0] = DAMPING * jnp.cos(angle)
    trig[1] = DAMPING * jnp.sin(angle)

    def turn(value, shift):
        shift %= LANES
        return pltpu.roll(value, shift, 1) if shift else value

    def span(t):
        return slice(t * LANES, (t + 1) * LANES)

    def set_factors(ext, t, diffusivity, wet):
        inverse = jnp.where(diffusivity > 0.0, 1.0 / jnp.where(diffusivity > 0.0, diffusivity, 1.0), 0.0)
        coupled = wet * diffusivity
        for i in range(8):
            d, w, v, u = (
                jnp.broadcast_to(x[i : i + 1], (8, LANES))
                for x in (diffusivity, wet, inverse, coupled)
            )
            sinus = w * trig[1]
            factor[0, ext + i, :, span(t)] = w * trig[0] - 4.0 * u
            factor[1, ext + i, :, span(t)] = sinus
            factor[2, ext + i, :, span(t)] = -sinus
            factor[3, ext + i, :, span(t)] = u
            factor[4, ext + i, :, span(t)] = v

    for load in loads[:2]:
        load.wait()
    coef[1] = ocean[...].astype(jnp.float32)
    for load in planes:
        load.wait()

    def prepare(block, carry):
        row = pl.multiple_of(block * 8, 8)
        for t in range(tiles):
            diffusivity = coef[0, pl.ds(row, 8), span(t)]
            for i in range(8):
                d = jnp.broadcast_to(diffusivity[i : i + 1], (8, LANES))
                for rh in range(GROUPS):
                    for p in range(2):
                        index = (rh, p, DEPTH + row + i, slice(None), span(t))
                        start[index] = d * start[index]
        return carry

    lax.fori_loop(0, rows // 8, prepare, 0)

    slot = lane // DEPTH

    def pack_half(rb, carry):
        row = rb * 16
        for g in range(2 * GROUPS + 1):
            to_west = jnp.zeros((8, LANES), jnp.float32)
            to_east = jnp.zeros((8, LANES), jnp.float32)
            for k in range(16 if g < 2 * GROUPS else 4):
                if g < 2 * GROUPS:
                    index = (g // 2, g % 2, DEPTH + row + k, slice(None))
                    left, right = start[index + (span(0),)], start[index + (span(tiles - 1),)]
                else:
                    some = pl.ds(row + 8 * (k % 2), 8)
                    left, right = coef[k // 2, some, span(0)], coef[k // 2, some, span(tiles - 1)]
                to_west = jnp.where(slot == k, turn(left, DEPTH * k), to_west)
                to_east = jnp.where(slot == k, turn(right, DEPTH * (k + 1)), to_east)
            pack[0, rb, g] = to_west
            pack[1, rb, g] = to_east
        return carry

    for rb in range(2):
        pack_half(rb, 0)

    mains, strips = (start, odd, even), (strip_start, strip_odd, strip_even)

    def sweep(refs, prefix, step, ext, count, widths, offset):
        src = refs[0] if step == 1 else refs[1 + step % 2]
        dst = refs[1 if step % 2 else 2]
        sign = 1 if step <= SWEEPS else 2
        value = [
            [
                [src[(*prefix, p, ext + i, slice(None), span(t))] for t in range(widths)]
                for p in range(2)
            ]
            for i in range(-1, count + 1)
        ]
        for i in range(count):
            around = []
            for p in range(2):
                here = value[i + 1][p]
                right = [pltpu.roll(v, 1, 1) for v in here]
                left = [pltpu.roll(v, LANES - 1, 1) for v in here]
                for t in range(widths):
                    w, e = right[t], left[t]
                    if t > 0:
                        w = jnp.where(lane == 0, right[t - 1], w)
                    if t < widths - 1:
                        e = jnp.where(lane == LANES - 1, left[t + 1], e)
                    around.append((value[i][p][t] + value[i + 2][p][t]) + (w + e))
            for t in range(widths):
                at_row = (ext + i, slice(None), span(t + offset))
                a, s, u = factor[(0, *at_row)], factor[(sign, *at_row)], factor[(3, *at_row)]
                real, imag = value[i + 1][0][t], value[i + 1][1][t]
                results = [
                    (a * real + s * imag) + u * around[t],
                    (a * imag - s * real) + u * around[widths + t],
                ]
                if step == SWEEPS:
                    results = [factor[(4, *at_row)] * v for v in results]
                for p in range(2):
                    dst[(*prefix, p, ext + i, slice(None), span(t))] = results[p]

    def main_rows(rh, step, ext, count):
        sweep(mains, (rh,), step, ext, count, tiles, 0)

    def strip_rows(step, ext, count):
        sweep(strips, (), step, ext, count, 1, tiles)

    def interior(step, size, body):
        chunks = (rows - 2 * step + size - 1) // size

        def one(k, carry):
            body(DEPTH + jnp.minimum(step + size * k, rows - size - step))
            return carry

        lax.fori_loop(0, chunks, one, 0)

    def interior_main(steps):
        for step in steps:

            def both(ext, step=step):
                for rh in range(GROUPS):
                    main_rows(rh, step, ext, 8)

            interior(step, 8, both)

    def main_factors(block, carry):
        row = pl.multiple_of(block * 8, 8)
        for t in range(tiles):
            set_factors(
                DEPTH + row, t, coef[0, pl.ds(row, 8), span(t)], coef[1, pl.ds(row, 8), span(t)]
            )
        return carry


    pl.semaphore_wait(barrier, len(sides) + 1)
    tell(0)

    def send(src, dst, sends, recvs, index, device):
        copy = pltpu.make_async_remote_copy(
            src, dst, sends.at[index], recvs.at[index], device_id=device, device_id_type=MESH
        )
        copy.start()
        return copy

    first, last = pl.ds(DEPTH, DEPTH), pl.ds(rows, DEPTH)
    head, tail = pl.ds(0, DEPTH), pl.ds(rows + DEPTH, DEPTH)
    lon_copies = [
        send(pack.at[0], east.at[pl.ds(1, 2)], lon_send, lon_recv, 0, at(-1, 0)),
        send(pack.at[1], west.at[pl.ds(1, 2)], lon_send, lon_recv, 1, at(1, 0)),
    ]
    coef_copies = [
        send(coef.at[:, last_rows], coef_lat.at[side], coef_send, coef_recv, side, at(0, hop))
        for side, (last_rows, hop) in enumerate(
            ((pl.ds(rows - DEPTH, DEPTH), 1), (pl.ds(0, DEPTH), -1))
        )
    ]
    lat_copies = []
    for rh in range(GROUPS):
        lat_copies.append(
            [
                send(
                    start.at[rh, p, src],
                    start.at[rh, p, dst],
                    lat_send,
                    lat_recv,
                    4 * rh + 2 * p + side,
                    at(0, hop),
                )
                for p in range(2)
                for side, (src, dst, hop) in enumerate(((last, head, 1), (first, tail, -1)))
            ]
        )

    lax.fori_loop(0, rows // 8, main_factors, 0)
    interior_main(range(1, SWEEPS + 1))
    learn(0)
    corner_copies = [
        send(pack.at[0, 1], east.at[0], lon_send, lon_recv, 2, at(-1, 1)),
        send(pack.at[0, 0], east.at[3], lon_send, lon_recv, 3, at(-1, -1)),
        send(pack.at[1, 1], west.at[0], lon_send, lon_recv, 4, at(1, 1)),
        send(pack.at[1, 0], west.at[3], lon_send, lon_recv, 5, at(1, -1)),
    ]
    tell(1)
    interior_main(range(SWEEPS + 1, DEPTH + 1))
    learn(1)
    tell(2)

    def strip_factors(block, main_of, valid):
        rb, half = (block + 1) // 2, (block + 1) % 2
        built = []
        for j in range(2):
            left, right = main_of(j, 0), main_of(j, tiles - 1)
            at_slot = DEPTH * (2 * j + half)
            value = jnp.where(lane < 48, turn(left, 32), 0.0)
            value = jnp.where(lane < 32, turn(west[rb, 2 * GROUPS], 24 - at_slot), value)
            value = jnp.where(lane < 24, turn(east[rb, 2 * GROUPS], 16 - at_slot), value)
            value = jnp.where(lane < 16, turn(right, 16), value)
            value = jnp.where(lane < 64, value, pltpu.roll(value, 64, 1))
            built.append(value if valid is None else jnp.where(valid, value, 0.0))
        set_factors(block * 8, tiles, *built)

    def strip_row(ext, rb, k, valid):
        for p in range(2):
            value = jnp.zeros((8, LANES), jnp.float32)
            for rh in range(GROUPS):
                base = 64 * rh
                index = (rh, p, ext, slice(None))
                part = jnp.where(lane < base + 48, turn(start[index + (span(0),)], base + 32), 0.0)
                part = jnp.where(
                    lane < base + 32, turn(west[rb, 2 * rh + p], base + 24 - DEPTH * k), part
                )
                part = jnp.where(
                    lane < base + 24, turn(east[rb, 2 * rh + p], base + 16 - DEPTH * k), part
                )
                part = jnp.where(
                    lane < base + 16, turn(start[index + (span(tiles - 1),)], base + 16), part
                )
                value = part if rh == 0 else jnp.where(lane < base, value, part)
            if valid is not None:
                value = jnp.where(valid, value, 0.0)
            strip_start[p, ext] = value

    def strip_body(rb, carry):
        for k in range(16):
            strip_row(DEPTH + rb * 16 + k, rb + 1, k, None)
        return carry

    loads[2].wait()
    loads[3].wait()
    loads[6].wait()
    live_slots = jnp.broadcast_to(count[...], (1, LANES))
    row_id = lax.broadcasted_iota(jnp.int32, (rows, LANES), 0)
    col_id = lax.broadcasted_iota(jnp.int32, (cols, LANES), 0)
    lane_1 = lax.broadcasted_iota(jnp.int32, (1, LANES), 1)

    def add_sites(j, total):
        cells = cell[pl.ds(j, 1), :]
        value = jnp.where(j * LANES + lane_1 < live_slots, weight[pl.ds(j, 1), :], 0.0)
        one = value.astype(jnp.bfloat16)
        rest = value - one.astype(jnp.float32)
        two = rest.astype(jnp.bfloat16)
        three = rest - two.astype(jnp.float32)
        hit_row = jnp.broadcast_to(cells // cols, (rows, LANES)) == row_id
        hit_col = jnp.broadcast_to(lax.rem(cells, cols), (cols, LANES)) == col_id
        terms = [
            jnp.where(hit_row, jnp.broadcast_to(term.astype(jnp.float32), (rows, LANES)), 0.0)
            for term in (one, two, three)
        ]
        lhs = jnp.concatenate(terms, axis=0).astype(jnp.bfloat16)
        rhs = jnp.where(hit_col, 1.0, 0.0).astype(jnp.bfloat16)
        return total + lax.dot_general(
            lhs, rhs, (((1,), (1,)), ((), ())), preferred_element_type=jnp.float32
        )

    summed = lax.fori_loop(
        0, cell.shape[0], add_sites, jnp.zeros((3 * rows, cols), jnp.float32)
    )
    summed = summed[:rows] + summed[rows : 2 * rows] + summed[2 * rows :]
    for row in range(rows):
        grid_w[row] = jnp.broadcast_to(summed[row : row + 1], (8, cols))

    for copy in lon_copies:
        copy.wait_recv()
    for block in range(1, 1 + rows // 8):
        strip_factors(
            block, lambda j, t, block=block: coef[j, pl.ds(8 * block - 8, 8), span(t)], None
        )
    lax.fori_loop(0, 2, strip_body, 0)
    for step in range(1, DEPTH + 1):
        interior(step, 16, lambda ext, step=step: strip_rows(step, ext, 16))

    def merge(first_row, length):
        for ext in range(DEPTH + first_row, DEPTH + first_row + length):
            for p in range(2):
                value = strip_even[p, ext]
                for rh in range(GROUPS):
                    left = even.at[rh, p, ext, :, span(0)]
                    right = even.at[rh, p, ext, :, span(tiles - 1)]
                    pltpu.store(left, turn(value, -32 - 64 * rh), mask=lane < DEPTH)
                    pltpu.store(
                        right, turn(value, LANES - 16 - 64 * rh), mask=lane >= LANES - DEPTH
                    )

    def share(rh, first_row, length, index):
        return send(
            even.at[rh, 1 - i_rep, pl.ds(DEPTH + first_row, length)],
            partner.at[rh, pl.ds(first_row, length)],
            part_send,
            part_recv,
            index,
            other,
        )

    merge(DEPTH, rows - 2 * DEPTH)
    parts = [share(rh, DEPTH, rows - 2 * DEPTH, rh) for rh in range(GROUPS)]

    learn(2)
    tell(3)
    acc[...] = jnp.zeros_like(acc)

    def own_rows(first_row, length):
        def one(block, totals):
            totals = list(totals)
            for row, p, t in [
                (first_row + 4 * block + i, p, t)
                for i in range(4)
                for p in range(2)
                for t in range(tiles)
            ]:
                values = [
                    even[rh, p, DEPTH + row, :, span(t)] for rh in range(GROUPS)
                ]
                scaled = [grid_w[row, :, span(t)] * v for v in values]
                turned = [pltpu.roll(v, 4, 0) for v in scaled]
                for j, (a, b) in enumerate(OWN_PAIRS):
                    totals[2 * j] += scaled[a] * values[b]
                    totals[2 * j + 1] += turned[a] * values[b]
            return tuple(totals)

        totals = lax.fori_loop(
            0, length // 4, one, tuple(acc[j] for j in range(6))
        )
        for j in range(6):
            acc[j] = totals[j]

    def cross_rows(first_row, length):
        def one(block, totals):
            totals = list(totals)
            for row, t in [
                (first_row + 4 * block + i, t) for i in range(4) for t in range(tiles)
            ]:
                scaled = [
                    grid_w[row, :, span(t)] * even[rh, i_rep, DEPTH + row, :, span(t)]
                    for rh in range(GROUPS)
                ]
                turned = [pltpu.roll(v, 4, 0) for v in scaled]
                values = [partner[rh, row, :, span(t)] for rh in range(GROUPS)]
                for j, (a, b) in enumerate(CROSS_PAIRS):
                    totals[2 * j] += scaled[a] * values[b]
                    totals[2 * j + 1] += turned[a] * values[b]
            return tuple(totals)

        totals = lax.fori_loop(
            0, length // 4, one, tuple(acc[6 + j] for j in range(8))
        )
        for j in range(8):
            acc[6 + j] = totals[j]

    own_rows(DEPTH, rows - 2 * DEPTH)
    for copy in parts:
        copy.wait_recv()
    cross_rows(DEPTH, rows - 2 * DEPTH)

    learn(3)
    north_in, south_in = i_lat > 0, i_lat < n_lat - 1
    for copy in coef_copies:
        copy.wait_recv()
    for side, (block, valid) in enumerate(((0, north_in), (ext_rows // 8 - 1, south_in))):
        for t in range(tiles):
            set_factors(
                8 * block,
                t,
                *(jnp.where(valid, coef_lat[side, j, :, span(t)], 0.0) for j in range(2)),
            )
    for copy in corner_copies:
        copy.wait_recv()
    for side, (block, valid) in enumerate(((0, north_in), (ext_rows // 8 - 1, south_in))):
        strip_factors(block, lambda j, t, side=side: coef_lat[side, j, :, span(t)], valid)
    for rh in range(GROUPS):
        for copy in lat_copies[rh]:
            copy.wait_recv()
        for ext, valid in ((DEPTH - 1, north_in), (rows + DEPTH, south_in)):
            for p in range(2):
                start[rh, p, ext] = jnp.where(valid, start[rh, p, ext], 0.0)
        if rh == GROUPS - 1:
            for i in range(DEPTH):
                strip_row(i, 0, DEPTH + i, north_in)
                strip_row(rows + DEPTH + i, 3, i, south_in)
        for step in range(1, DEPTH + 1):
            for ext in (step, rows + DEPTH - step):
                main_rows(rh, step, ext, DEPTH)
                if rh == GROUPS - 1:
                    strip_rows(step, ext, DEPTH)
    merge(0, DEPTH)
    merge(rows - DEPTH, DEPTH)
    late = []
    for rh in range(GROUPS):
        late.append(share(rh, 0, DEPTH, 2 + 2 * rh))
        late.append(share(rh, rows - DEPTH, DEPTH, 3 + 2 * rh))
    stores = [
        pltpu.make_async_copy(
            even.at[rh, p, own, m], rep_out.at[16 * rh + 2 * m + p], out_sem.at[rh, p, m]
        )
        for rh in range(GROUPS)
        for p in range(2)
        for m in range(8)
    ]
    own_rows(0, DEPTH)
    own_rows(rows - DEPTH, DEPTH)
    for copy in late:
        copy.wait_recv()
    cross_rows(0, DEPTH)
    cross_rows(rows - DEPTH, DEPTH)

    packed = jnp.zeros((8, LANES), jnp.float32)
    for j in range(14):
        packed = jnp.where(lane == j, jnp.sum(acc[j], axis=1, keepdims=True), packed)
    packed = packed + pltpu.roll(packed, 7, 0)
    packed = packed + pltpu.roll(packed, 6, 0)
    second = pltpu.roll(pltpu.roll(packed, 4, 0), 16, 1)
    packed = jnp.where(lane < 16, packed, second)
    packed = jnp.where(i_rep == 0, packed, pltpu.roll(packed, 32, 1))

    def sum_start(row, buffer, me, size, peer, targets, sends, recvs):
        buffer[me] = row
        for target in targets:
            copy = pltpu.make_async_remote_copy(
                buffer.at[me],
                buffer.at[me],
                sends,
                recvs,
                device_id=peer(target),
                device_id_type=MESH,
            )
            copy.start()

    def sum_end(buffer, me, size, peer, targets, sends, recvs):
        several = buffer.at[pl.ds(0, size - 1)]
        pltpu.make_async_remote_copy(
            several, several, sends, recvs, device_id=peer(targets[0]), device_id_type=MESH
        ).wait_recv()
        total = buffer[0]
        for k in range(1, size):
            total = total + buffer[k]
        return total

    def sum_sent(buffer, me, size, peer, targets, sends, recvs):
        several = buffer.at[pl.ds(0, size - 1)]
        pltpu.make_async_remote_copy(
            several, several, sends, recvs, device_id=peer(targets[0]), device_id_type=MESH
        ).wait_send()

    first_sum = (stage1, me1, size1, peer1, others1, sum1_send, sum1_recv)
    second_sum = (stage2, me2, size2, peer2, others2, sum2_send, sum2_recv)
    sum_start(packed[0:1], *first_sum)
    for store in stores:
        store.start()
    for copy in lon_copies + coef_copies + corner_copies + parts + late:
        copy.wait_send()
    for some in lat_copies:
        for copy in some:
            copy.wait_send()
    loads[4].wait()
    row = sum_end(*first_sum)
    sum_start(row, *second_sum)
    sum_sent(*first_sum)
    for store in stores:
        store.wait()
    row = sum_end(*second_sum)

    row = jnp.broadcast_to(row, (8, LANES))
    result = jnp.zeros((8, LANES), jnp.float32)
    for q in range(8):
        result = jnp.where(
            lane == q, jnp.sum(row * masks[i_rep, q], axis=1, keepdims=True), result
        )
    gram_out[...] = result[0:4, 0:8]

    sum_sent(*second_sum)


def local(n_lon, n_lat, forcing, diffusivity, ocean, phase, site_cell, site_count, site_weight):
    reps, const, parts, rows, cols = forcing.shape
    planes = reps * const * parts
    slots = site_cell.shape[2]
    masks = jnp.asarray(entry_masks(float(n_lon * n_lat * slots)))
    ext = rows + 2 * DEPTH
    wide = cols + LANES
    any_space = pl.BlockSpec(memory_space=pl.ANY)
    vmem = pl.BlockSpec(memory_space=pltpu.VMEM)
    f32 = jnp.float32
    dma = pltpu.SemaphoreType.DMA
    size1, size2 = n_lat, 2 * n_lon
    representer, gram = pl.pallas_call(
        functools.partial(kernel, n_lon, n_lat),
        out_shape=(
            jax.ShapeDtypeStruct((planes, rows, cols), f32),
            jax.ShapeDtypeStruct((reps, 2 * reps), f32),
        ),
        in_specs=[any_space] * 8,
        out_specs=(any_space, vmem),
        scratch_shapes=[
            *[pltpu.VMEM((GROUPS, 2, ext, 8, cols), f32)] * 3,
            *[pltpu.VMEM((2, ext, 8, LANES), f32)] * 3,
            pltpu.VMEM((2, 2, 2 * GROUPS + 1, 8, LANES), f32),
            pltpu.VMEM((4, 2 * GROUPS + 1, 8, LANES), f32),
            pltpu.VMEM((4, 2 * GROUPS + 1, 8, LANES), f32),
            pltpu.VMEM((2, rows, cols), f32),
            pltpu.VMEM((rows, cols), jnp.int32),
            pltpu.VMEM((2, 2, DEPTH, cols), f32),
            pltpu.VMEM((5, ext, 8, wide), f32),
            pltpu.VMEM((2, 8, LANES), f32),
            pltpu.VMEM((slots // LANES, LANES), jnp.int32),
            pltpu.VMEM((slots // LANES, LANES), f32),
            pltpu.VMEM(masks.shape, f32),
            pltpu.VMEM((1, CONST), f32),
            pltpu.VMEM((1, 1), jnp.int32),
            pltpu.VMEM((rows, 8, cols), f32),
            pltpu.VMEM((GROUPS, rows, 8, cols), f32),
            pltpu.VMEM((14, 8, LANES), f32),
            pltpu.VMEM((size1, 1, LANES), f32),
            pltpu.VMEM((size2, 1, LANES), f32),
            pltpu.SemaphoreType.REGULAR((4,)),
            dma((7,)),
            dma((GROUPS, 2, 8)),
            dma((GROUPS, 2, 8)),
            dma((8,)),
            dma((8,)),
            dma((6,)),
            dma((6,)),
            dma((2,)),
            dma((2,)),
            dma((6,)),
            dma((6,)),
            dma,
            dma,
            dma,
            dma,
        ],
        compiler_params=pltpu.CompilerParams(
            collective_id=0, has_side_effects=True, vmem_limit_bytes=40 << 20
        ),
        name="representer_block",
    )(
        *[
            pltpu.with_memory_space_constraint(x, pltpu.HBM)
            for x in (
                forcing.reshape(planes, rows, cols),
                diffusivity,
                ocean,
                site_cell.reshape(slots // LANES, LANES),
                site_weight.reshape(slots // LANES, LANES),
                masks,
                phase.reshape(1, CONST),
            )
        ],
        site_count,
    )
    return representer.reshape(forcing.shape), gram


def solution(mesh):
    return jax.shard_map(
        functools.partial(local, mesh.shape["lon"], mesh.shape["lat"]),
        mesh=mesh,
        in_specs=(
            P("rep", None, None, "lat", "lon"),
            P("lat", "lon"),
            P("lat", "lon"),
            P(),
            P("lat", "lon", None),
            P("lat", "lon"),
            P("lat", "lon", None),
        ),
        out_specs=(P("rep", None, None, "lat", "lon"), P("rep", None)),
        check_vma=False,
    )
```
